128 devices in a mesh: ctx: 32 (over x, y, z_hi), head: 4 (over z_lo, core).
Axes of the slice: x: 4, y: 4, z: 4 (z_hi: 2, z_lo: 2; z = z_hi * 2 + z_lo), core: 2. Of those that a mesh axis runs over, the one named last changes fastest.
Arguments:
- hidden: bfloat16 [16384, 5376], P('ctx'), may hold values from -18 to 18
- w_query: bfloat16 [5376, 2048], P(None, 'head'), may hold values from -0.078125 to 0.078125
- key_weight_matrix: bfloat16 [5376, 1024], P(None, 'head'), may hold values from -0.078125 to 0.078125
- value_weight_matrix: bfloat16 [5376, 1024], P(None, 'head'), may hold values from -0.078125 to 0.078125
- attention_output_gradient: bfloat16 [16384, 2048], P('ctx', 'head'), may hold values from -6 to 6
- doc_start: int32 [16384], P('ctx'), may hold values from 0 to 16383, as said below
Outputs:
- d_hidden: float32 [16384, 5376], P(('ctx', 'head'))
The draws below stay inside these ranges and needn't reach their ends.
Inputs may be any that keep to these rules, and one draw needn't show every extreme that they name: doc_start is non-decreasing, doc_start[i] <= i, constant within a document and equal to i at a document's first token; doc_start[0] = 0, and the last token begins a document of its own.
All inputs are finite; a program needn't handle non-finite values.
Results may differ from the reference program's by a relative error of at most 0.014.
The reference program's roundings to bfloat16 on the way (of `probability_low`, `d_scores` and `d_query`) count: a program that leaves them out, or rounds other values in their place, can miss the bound.
Values may be sent and summed in bfloat16 or wider, within the bound.
A program may use at most 128 MiB of HBM per device.

```python
import jax
import jax.numpy as jnp
from jax import lax

MODEL_WIDTH = 5376
QUERY_HEADS = 16
KEY_VALUE_HEADS = 8
HEAD_SIZE = 128
W = 1024
LOCAL_TOKENS = 512
SEQUENCE_TOKENS = 16384
HALO = 2


def draw_hidden(key, part):
    first_key = jax.random.fold_in(key, 11)
    entries = jnp.clip(jax.random.normal(first_key, (SEQUENCE_TOKENS, MODEL_WIDTH), jnp.float32), -4.0, 4.0)
    return entries.astype(jnp.bfloat16)


def draw_doc_start(key, part):
    marks = jax.random.randint(jax.random.fold_in(key, 21), (SEQUENCE_TOKENS,), 0, 4 * W)
    positions = jnp.arange(SEQUENCE_TOKENS, dtype=jnp.int32)
    opening = (marks == 0) | (positions == 0) | (positions == SEQUENCE_TOKENS - 1)
    starts = jnp.where(opening, positions, 0).astype(jnp.int32)
    return lax.cummax(starts, axis=0)


def level_of(own_key, extent, cuts, least, largest):
    level, own = 1.0, jax.random.fold_in(own_key, 6)
    for axis_at, shards_of in cuts:
        draws = jnp.exp(jax.random.uniform(jax.random.fold_in(own, axis_at), (shards_of,), jnp.float32, least / len(cuts), largest / len(cuts)))
        level = level * jnp.repeat(draws, extent[axis_at] // shards_of).reshape([-1 if axis == axis_at else 1 for axis in range(len(extent))])
    return level


def gaussian(own_key, dims, scale, reach, cuts=(), kind=jnp.bfloat16):
    level = level_of(own_key, dims, cuts, -0.22, 0.18) if cuts else 1.0
    values = jax.random.normal(own_key, dims, jnp.float32) * scale * level
    return jnp.minimum(jnp.maximum(values, -reach), reach).astype(kind)


def setup_inputs(seed: int = 0) -> dict:
    arg_keys = jax.random.split(jax.random.key(seed), 7)
    hidden = draw_hidden(jax.random.fold_in(arg_keys[6], 71), 0)
    w_query = gaussian(arg_keys[1], (MODEL_WIDTH, QUERY_HEADS * HEAD_SIZE), MODEL_WIDTH ** -0.5, 0.078125, ((1, 4),))
    key_weight_matrix = gaussian(arg_keys[2], (MODEL_WIDTH, KEY_VALUE_HEADS * HEAD_SIZE), MODEL_WIDTH ** -0.5, 0.078125, ((1, 4),))
    value_weight_matrix = gaussian(arg_keys[3], (MODEL_WIDTH, KEY_VALUE_HEADS * HEAD_SIZE), MODEL_WIDTH ** -0.5, 0.078125, ((1, 4),))
    attention_output_gradient = gaussian(arg_keys[4], (SEQUENCE_TOKENS, QUERY_HEADS * HEAD_SIZE), 1.0, 6.0, ((0, 32), (1, 4)))
    doc_start = draw_doc_start(jax.random.fold_in(arg_keys[6], 71), 0)
    return dict(hidden=hidden, w_query=w_query, key_weight_matrix=key_weight_matrix, value_weight_matrix=value_weight_matrix, attention_output_gradient=attention_output_gradient, doc_start=doc_start)


SCALE = 168.0 ** -0.5


def masked_scores(query_rows, key_tile_block, query_position, lower_bound, key_position):
    scores = jnp.einsum("ikgd,jkd->kgij", query_rows.astype(jnp.float32), key_tile_block.astype(jnp.float32)) * SCALE
    allowed = (key_position[None, :] >= lower_bound[:, None]) & (key_position[None, :] <= query_position[:, None])
    return jnp.where(allowed[None, None], scores, -jnp.inf)


def block_backward(query_rows, output_gradient, key_tile_block, value_tile_block, query_position, lower_bound, key_position):
    scores = masked_scores(query_rows, key_tile_block, query_position, lower_bound, key_position)
    row_max = jnp.max(scores, axis=-1, keepdims=True)
    denominator = jnp.sum(jnp.exp(scores - row_max), axis=-1, keepdims=True)
    probability = jnp.exp(scores - (row_max + jnp.log(denominator)))
    probability_low = probability.astype(jnp.bfloat16)
    output = jnp.einsum("kgij,jkd->ikgd", probability_low.astype(jnp.float32), value_tile_block.astype(jnp.float32))
    row_dot = jnp.einsum("ikgd,ikgd->kgi", output_gradient.astype(jnp.float32), output)
    d_probs = jnp.einsum("ikgd,jkd->kgij", output_gradient.astype(jnp.float32), value_tile_block.astype(jnp.float32))
    d_scores = (probability * (d_probs - row_dot[..., None]) * SCALE).astype(jnp.bfloat16)
    d_query = jnp.einsum("kgij,jkd->ikgd", d_scores.astype(jnp.float32), key_tile_block.astype(jnp.float32))
    d_key = jnp.einsum("kgij,ikgd->jkd", d_scores.astype(jnp.float32), query_rows.astype(jnp.float32))
    d_value = jnp.einsum("kgij,ikgd->jkd", probability_low.astype(jnp.float32), output_gradient.astype(jnp.float32))
    return d_query, d_key, d_value


def back_project(grad, weight):
    return lax.dot_general(grad, weight, (((1,), (1,)), ((), ())), preferred_element_type=jnp.float32)


def reference(hidden, w_query, key_weight_matrix, value_weight_matrix, attention_output_gradient, doc_start):
    query_group_count = QUERY_HEADS // KEY_VALUE_HEADS
    query_rows = jnp.dot(hidden, w_query, preferred_element_type=jnp.float32).astype(jnp.bfloat16)
    projected_keys = jnp.dot(hidden, key_weight_matrix, preferred_element_type=jnp.float32).astype(jnp.bfloat16)
    projected_values = jnp.dot(hidden, value_weight_matrix, preferred_element_type=jnp.float32).astype(jnp.bfloat16)
    padding_rows = HALO * LOCAL_TOKENS
    covered_rows = (HALO + 1) * LOCAL_TOKENS
    padded_keys = jnp.concatenate([jnp.zeros((padding_rows, KEY_VALUE_HEADS * HEAD_SIZE), jnp.bfloat16), projected_keys], axis=0)
    padded_values = jnp.concatenate([jnp.zeros((padding_rows, KEY_VALUE_HEADS * HEAD_SIZE), jnp.bfloat16), projected_values], axis=0)
    positions = jnp.arange(SEQUENCE_TOKENS, dtype=jnp.int32)
    lower_all = jnp.maximum(doc_start, positions - W + 1)

    def attend_block(running, block_index):
        d_key_all, d_value_all = running
        leading_row = (block_index * LOCAL_TOKENS).astype(jnp.int32)
        query_tile_block = lax.dynamic_slice_in_dim(query_rows, leading_row, LOCAL_TOKENS, 0).reshape(LOCAL_TOKENS, KEY_VALUE_HEADS, query_group_count, HEAD_SIZE)
        output_gradient = lax.dynamic_slice_in_dim(attention_output_gradient, leading_row, LOCAL_TOKENS, 0).reshape(LOCAL_TOKENS, KEY_VALUE_HEADS, query_group_count, HEAD_SIZE)
        key_tile_block = lax.dynamic_slice_in_dim(padded_keys, leading_row, covered_rows, 0).reshape(covered_rows, KEY_VALUE_HEADS, HEAD_SIZE)
        value_tile_block = lax.dynamic_slice_in_dim(padded_values, leading_row, covered_rows, 0).reshape(covered_rows, KEY_VALUE_HEADS, HEAD_SIZE)
        query_position = leading_row + jnp.arange(LOCAL_TOKENS, dtype=jnp.int32)
        lower_bound = lax.dynamic_slice_in_dim(lower_all, leading_row, LOCAL_TOKENS, 0)
        key_position = leading_row - padding_rows + jnp.arange(covered_rows, dtype=jnp.int32)
        d_query, d_key, d_value = block_backward(query_tile_block, output_gradient, key_tile_block, value_tile_block, query_position, lower_bound, key_position)
        d_key_all = lax.dynamic_update_slice_in_dim(d_key_all, lax.dynamic_slice_in_dim(d_key_all, leading_row, covered_rows, 0) + d_key, leading_row, 0)
        d_value_all = lax.dynamic_update_slice_in_dim(d_value_all, lax.dynamic_slice_in_dim(d_value_all, leading_row, covered_rows, 0) + d_value, leading_row, 0)
        return (d_key_all, d_value_all), d_query.reshape(LOCAL_TOKENS, QUERY_HEADS * HEAD_SIZE)

    initial_state = (jnp.zeros((SEQUENCE_TOKENS + padding_rows, KEY_VALUE_HEADS, HEAD_SIZE), jnp.float32), jnp.zeros((SEQUENCE_TOKENS + padding_rows, KEY_VALUE_HEADS, HEAD_SIZE), jnp.float32))
    closing_state, d_query_blocks = lax.scan(attend_block, initial_state, jnp.arange(SEQUENCE_TOKENS // LOCAL_TOKENS, dtype=jnp.int32))
    d_query = d_query_blocks.reshape(SEQUENCE_TOKENS, QUERY_HEADS * HEAD_SIZE).astype(jnp.bfloat16)
    key_gradient_rows = closing_state[0][padding_rows:].reshape(SEQUENCE_TOKENS, KEY_VALUE_HEADS * HEAD_SIZE).astype(jnp.bfloat16)
    value_gradient_rows = closing_state[1][padding_rows:].reshape(SEQUENCE_TOKENS, KEY_VALUE_HEADS * HEAD_SIZE).astype(jnp.bfloat16)
    summed = back_project(d_query, w_query)
    summed = summed + back_project(key_gradient_rows, key_weight_matrix)
    summed = summed + back_project(value_gradient_rows, value_weight_matrix)
    return summed
```

```python
import functools
import math

import jax
import jax.numpy as jnp
from jax import lax
from jax.experimental import pallas as pl
from jax.experimental.pallas import tpu as pltpu
from jax.sharding import PartitionSpec as P

HEAD = 128
WINDOW = 1024
SCALE = 168.0 ** (-0.5)
LOG2E = math.log2(math.e)
MESH = pl.DeviceIdType.MESH
F32 = jnp.float32
BF16 = jnp.bfloat16

TOK = 512
QT = 256
KEYS = 1280
STRIP = 32
NT = (((1,), (1,)), ((), ()))
TN = (((0,), (0,)), ((), ()))


def kernel(
    n_ctx, kcn, kc, ncn, nc,
    hid, wq, wk, wv, dog, doc, out,
    h, wall, acc, kv, q, do, lo, s, dp, pw, ds, dkv, dkv_out, dkv_in, grad,
    rs1_out, rs1_in, rs2_out, rs2_in, other, keep,
    sem_h, sem_k, sem_v, sem_q, sem_do, sem_o,
    kv_ss, kv_rs, dkv_ss, dkv_rs, r1_ss, r1_rs, r2_ss, r2_rs,
):
    ctx = lax.axis_index("ctx")
    head = lax.axis_index("head")
    zpos, core = head // 2, lax.rem(head, 2)

    def at_ctx(by):
        return (lax.rem(ctx + by + n_ctx, n_ctx), head)

    next1, next2, prev1, prev2 = at_ctx(1), at_ctx(2), at_ctx(-1), at_ctx(-2)
    mate = (ctx, head + 1 - 2 * core)
    across = (ctx, lax.rem(head + 2, 4))

    barrier = pltpu.get_barrier_semaphore()
    for peer in (next1, next2, prev1, prev2, mate, across):
        pl.semaphore_signal(barrier, inc=1, device_id=peer, device_id_type=MESH)

    def cols(k):
        return pl.ds(pl.multiple_of(k * kc, 128), kc)

    def in_h(k):
        return pltpu.make_async_copy(hid.at[:, cols(k)], h.at[k], sem_h.at[k])

    def in_k(k):
        return pltpu.make_async_copy(wk.at[cols(k), :], wall.at[cols(k), pl.ds(512, 256)], sem_k.at[k])

    def in_v(k):
        return pltpu.make_async_copy(wv.at[cols(k), :], wall.at[cols(k), pl.ds(768, 256)], sem_v.at[k])

    def in_q(k):
        return pltpu.make_async_copy(wq.at[cols(k), :], wall.at[cols(k), pl.ds(0, 512)], sem_q.at[k])

    for k in range(kcn):
        in_h(k).start()
        in_k(k).start()
        in_v(k).start()
    for k in range(kcn):
        in_q(k).start()
    do_copies = []
    for g in range(2):
        for t in range(2):
            for m in range(2):
                do_copies.append(
                    pltpu.make_async_copy(
                        dog.at[pl.ds(t * QT, QT), pl.ds((2 * g + m) * HEAD, HEAD)],
                        do.at[g, t, pl.ds(m * QT, QT), :],
                        sem_do.at[4 * g + 2 * t + m],
                    )
                )
    for copy in do_copies:
        copy.start()

    first = ctx * TOK
    lane = lax.broadcasted_iota(jnp.int32, (1, TOK), 1)
    low = jnp.maximum(doc[...].reshape(1, TOK) - first + WINDOW, lane + 1)
    for t in range(2):
        part = low[:, t * QT : (t + 1) * QT] - t * QT
        lo[t] = jnp.concatenate([part, part], axis=1)

    acc[...] = jnp.zeros_like(acc)

    @pl.loop(0, kcn)
    def _(k):
        in_h(k).wait()
        in_k(k).wait()
        in_v(k).wait()
        acc[...] += jnp.dot(h[k], wall[cols(k), pl.ds(512, 512)], preferred_element_type=F32)

    for g in range(2):
        for j in range(2):
            kv[g, j, pl.ds(2 * TOK, TOK), :] = acc[:, pl.ds(j * 256 + g * HEAD, HEAD)].astype(BF16)

    pl.semaphore_wait(barrier, 6)

    def send_kv(g, far):
        return pltpu.make_async_remote_copy(
            src_ref=kv.at[g, :, pl.ds(2 * TOK, TOK), :],
            dst_ref=kv.at[g, :, pl.ds((1 - far) * TOK, TOK), :],
            send_sem=kv_ss.at[g, far],
            recv_sem=kv_rs.at[g, far],
            device_id=next2 if far else next1,
            device_id_type=MESH,
        )

    for g in range(2):
        for far in range(2):
            send_kv(g, far).start()

    acc[...] = jnp.zeros_like(acc)

    @pl.loop(0, kcn)
    def _(k):
        in_q(k).wait()
        acc[...] += jnp.dot(h[k], wall[cols(k), pl.ds(0, 512)], preferred_element_type=F32)

    for g in range(2):
        for t in range(2):
            for m in range(2):
                q[g, t, pl.ds(m * QT, QT), :] = acc[
                    pl.ds(t * QT, QT), pl.ds((2 * g + m) * HEAD, HEAD)
                ].astype(BF16)
    for copy in do_copies:
        copy.wait()
    dkv[...] = jnp.zeros_like(dkv)

    def same(a, b):
        return 1 - (a + b - 2 * a * b)

    def place(b):
        return pl.multiple_of(128 * (2 * same(lax.rem(b, 2), core) + same(b // 2, zpos)), 128)

    def send_dkv(g, far):
        return pltpu.make_async_remote_copy(
            src_ref=dkv_out.at[g, :, pl.ds((1 - far) * TOK, TOK), :],
            dst_ref=dkv_in.at[far, g],
            send_sem=dkv_ss.at[g, far],
            recv_sem=dkv_rs.at[g, far],
            device_id=prev2 if far else prev1,
            device_id_type=MESH,
        )

    for g in range(2):
        for far in range(2):
            send_kv(g, far).wait_recv()

        @pl.loop(0, 2)
        def _(t):
            rows = pl.ds(pl.multiple_of(t * QT, QT), KEYS)
            s[...] = lax.dot_general(kv[g, 0, rows, :], q[g, t], NT, preferred_element_type=F32)
            dp[...] = lax.dot_general(kv[g, 1, rows, :], do[g, t], NT, preferred_element_type=F32)
            lowest = lo[t]
            local = lax.broadcasted_iota(jnp.int32, (STRIP, 2 * QT), 0)
            lane2 = lax.broadcasted_iota(jnp.int32, (1, QT), 1)
            highest = WINDOW + jnp.concatenate([lane2, lane2], axis=1)

            def strip(i):
                return pl.ds(pl.multiple_of(i * STRIP, STRIP), STRIP)

            def mask_inner(i, top):
                kept = jnp.where(local + i * STRIP >= lowest, s[strip(i), :], -jnp.inf)
                s[strip(i), :] = kept
                return jnp.maximum(top, kept)

            def mask_edge(i, top):
                key = local + i * STRIP
                kept = jnp.where((key >= lowest) & (key <= highest), s[strip(i), :], -jnp.inf)
                s[strip(i), :] = kept
                return jnp.maximum(top, kept)

            top = jnp.full((STRIP, 2 * QT), -jnp.inf, F32)
            top = lax.fori_loop(0, WINDOW // STRIP, mask_inner, top)
            top = lax.fori_loop(WINDOW // STRIP, KEYS // STRIP, mask_edge, top)
            top = jnp.max(top, axis=0, keepdims=True)

            def weigh(i, sums):
                total, dots = sums
                weight = jnp.exp2((s[strip(i), :] - top) * (SCALE * LOG2E))
                s[strip(i), :] = weight
                return total + weight, dots + weight * dp[strip(i), :]

            zero = jnp.zeros((STRIP, 2 * QT), F32)
            total, dots = lax.fori_loop(0, KEYS // STRIP, weigh, (zero, zero))
            inverse = 1.0 / jnp.sum(total, axis=0, keepdims=True)
            row_dot = jnp.sum(dots, axis=0, keepdims=True) * inverse

            @pl.loop(0, KEYS // STRIP)
            def _(i):
                prob = s[strip(i), :] * inverse
                pw[strip(i), :] = prob.astype(BF16)
                ds[strip(i), :] = (prob * (dp[strip(i), :] - row_dot)).astype(BF16)

            dq = lax.dot_general(kv[g, 0, rows, :], ds[...], TN, preferred_element_type=F32)
            dq = jnp.transpose(dq * SCALE).astype(BF16)
            for m in range(2):
                for j in range(2):
                    grad[pl.ds(place(2 * t + j), 128), pl.ds((2 * g + m) * HEAD, HEAD)] = dq[
                        m * QT + j * 128 : m * QT + (j + 1) * 128
                    ]
            dkv[g, 0, rows, :] += jnp.dot(ds[...], q[g, t], preferred_element_type=F32)
            dkv[g, 1, rows, :] += jnp.dot(pw[...], do[g, t], preferred_element_type=F32)

        dkv_out[g, 0] = (dkv[g, 0, pl.ds(0, 2 * TOK), :] * SCALE).astype(BF16)
        dkv_out[g, 1] = dkv[g, 1, pl.ds(0, 2 * TOK), :].astype(BF16)
        for far in range(2):
            send_dkv(g, far).start()

    for g in range(2):
        for far in range(2):
            send_dkv(g, far).wait_recv()
        for j in range(2):
            for b in range(4):
                rows = pl.ds(b * 128, 128)
                own = dkv[g, j, pl.ds(2 * TOK + b * 128, 128), :]
                if j == 0:
                    own = own * SCALE
                whole = own + (dkv_in[0, g, j, rows, :].astype(F32) + dkv_in[1, g, j, rows, :].astype(F32))
                grad[pl.ds(place(b), 128), pl.ds(512 + j * 256 + g * HEAD, HEAD)] = whole.astype(BF16)

    def send_r1(c):
        return pltpu.make_async_remote_copy(
            src_ref=rs1_out.at[c], dst_ref=rs1_in.at[c],
            send_sem=r1_ss.at[c], recv_sem=r1_rs.at[c],
            device_id=mate, device_id_type=MESH,
        )

    def send_r2(c):
        return pltpu.make_async_remote_copy(
            src_ref=rs2_out.at[c], dst_ref=rs2_in.at[c],
            send_sem=r2_ss.at[c], recv_sem=r2_rs.at[c],
            device_id=across, device_id_type=MESH,
        )

    def out_copy(c):
        return pltpu.make_async_copy(
            keep.at[c], out.at[:, pl.ds(pl.multiple_of(c * nc, nc), nc)], sem_o.at[c]
        )

    def join(c):
        send_r1(c).wait_recv()
        rs2_out[c] = (other[c] + rs1_in[c, pl.ds(0, 128), :].astype(F32)).astype(BF16)
        send_r2(c).start()
        keep[c] = keep[c] + rs1_in[c, pl.ds(128, 128), :].astype(F32)

    @pl.loop(0, ncn)
    def _(c):
        part = lax.dot_general(
            grad[...], wall[pl.ds(pl.multiple_of(c * nc, nc), nc), :], NT, preferred_element_type=F32
        )
        rs1_out[c] = part[:256].astype(BF16)
        other[c] = part[256:384]
        keep[c] = part[384:]
        send_r1(c).start()

        @pl.when(c > 0)
        def _():
            join(c - 1)

    join(ncn - 1)

    @pl.loop(0, ncn)
    def _(c):
        send_r2(c).wait_recv()
        keep[c] = keep[c] + rs2_in[c].astype(F32)
        out_copy(c).start()

    @pl.loop(0, ncn)
    def _(c):
        out_copy(c).wait()
        send_r1(c).wait_send()
        send_r2(c).wait_send()

    for g in range(2):
        for far in range(2):
            send_kv(g, far).wait_send()
            send_dkv(g, far).wait_send()


def shards(hidden, w_query, key_weight, value_weight, out_gradient, doc_start, *, n_ctx):
    width = hidden.shape[1]
    kcn = 7
    kc = width // kcn
    nc = 256
    ncn = width // nc
    dma = pltpu.SemaphoreType.DMA
    anywhere = pl.BlockSpec(memory_space=pl.ANY)
    return pl.pallas_call(
        functools.partial(kernel, n_ctx, kcn, kc, ncn, nc),
        out_shape=jax.ShapeDtypeStruct((128, width), F32),
        in_specs=[anywhere] * 5 + [pl.BlockSpec(memory_space=pltpu.VMEM)],
        out_specs=anywhere,
        scratch_shapes=[
            pltpu.VMEM((kcn, TOK, kc), BF16),
            pltpu.VMEM((width, 1024), BF16),
            pltpu.VMEM((TOK, TOK), F32),
            pltpu.VMEM((2, 2, 3 * TOK, HEAD), BF16),
            pltpu.VMEM((2, 2, 2 * QT, HEAD), BF16),
            pltpu.VMEM((2, 2, 2 * QT, HEAD), BF16),
            pltpu.VMEM((2, 1, 2 * QT), jnp.int32),
            pltpu.VMEM((KEYS, 2 * QT), F32),
            pltpu.VMEM((KEYS, 2 * QT), F32),
            pltpu.VMEM((KEYS, 2 * QT), BF16),
            pltpu.VMEM((KEYS, 2 * QT), BF16),
            pltpu.VMEM((2, 2, 3 * TOK, HEAD), F32),
            pltpu.VMEM((2, 2, 2 * TOK, HEAD), BF16),
            pltpu.VMEM((2, 2, 2, TOK, HEAD), BF16),
            pltpu.VMEM((TOK, 1024), BF16),
            pltpu.VMEM((ncn, 256, nc), BF16),
            pltpu.VMEM((ncn, 256, nc), BF16),
            pltpu.VMEM((ncn, 128, nc), BF16),
            pltpu.VMEM((ncn, 128, nc), BF16),
            pltpu.VMEM((ncn, 128, nc), F32),
            pltpu.VMEM((ncn, 128, nc), F32),
            dma((kcn,)), dma((kcn,)), dma((kcn,)), dma((kcn,)), dma((8,)), dma((ncn,)),
            dma((2, 2)), dma((2, 2)), dma((2, 2)), dma((2, 2)),
            dma((ncn,)), dma((ncn,)), dma((ncn,)), dma((ncn,)),
        ],
        compiler_params=pltpu.CompilerParams(
            collective_id=0, has_side_effects=True, vmem_limit_bytes=60 * 1024 * 1024
        ),
    )(hidden, w_query, key_weight, value_weight, out_gradient, doc_start)


def solution(mesh):
    in_specs = (
        P("ctx", None),
        P(None, "head"),
        P(None, "head"),
        P(None, "head"),
        P("ctx", "head"),
        P("ctx"),
    )
    out_specs = P(("ctx", "head"), None)
    return jax.shard_map(
        functools.partial(shards, n_ctx=mesh.shape["ctx"]),
        mesh=mesh, in_specs=in_specs, out_specs=out_specs, check_vma=False,
    )
```

```python
import functools
import math

import jax
import jax.numpy as jnp
from jax import lax
from jax.experimental import pallas as pl
from jax.experimental.pallas import tpu as pltpu
from jax.sharding import PartitionSpec as P

HEAD = 128
WINDOW = 1024
SCALE = 168.0 ** (-0.5)
LOG2E = math.log2(math.e)
MESH = pl.DeviceIdType.MESH
F32 = jnp.float32
BF16 = jnp.bfloat16

TOK = 512
QT = 256
KEYS = 1280
CH = 256
NT = (((1,), (1,)), ((), ()))
TN = (((0,), (0,)), ((), ()))


def kernel(
    n_ctx, kcn, kc, ncn, nc,
    hid, wq, wk, wv, dog, doc, out, rs2_in,
    h, wall, acc, kv, q, do, lo, s, dp, pw, ds, dkv, dkv_out, dkv_in, grad,
    rs1_out, rs1_in, rs2_out, other, keep,
    sem_h, sem_k, sem_v, sem_q, sem_do, sem_o,
    kv_ss, kv_rs, dkv_ss, dkv_rs, r1_ss, r1_rs, r2_ss, r2_rs,
):
    ctx = lax.axis_index("ctx")
    head = lax.axis_index("head")
    zpos, core = head // 2, lax.rem(head, 2)

    def at_ctx(by):
        return (lax.rem(ctx + by + n_ctx, n_ctx), head)

    next1, next2, prev1, prev2 = at_ctx(1), at_ctx(2), at_ctx(-1), at_ctx(-2)
    mate = (ctx, head + 1 - 2 * core)
    across = (ctx, lax.rem(head + 2, 4))

    barrier = pltpu.get_barrier_semaphore()
    for peer in (next1, next2, prev1, prev2, mate, across):
        pl.semaphore_signal(barrier, inc=1, device_id=peer, device_id_type=MESH)

    def cols(k):
        return pl.ds(pl.multiple_of(k * kc, 128), kc)

    def in_h(k):
        return pltpu.make_async_copy(hid.at[:, cols(k)], h.at[k], sem_h.at[k])

    def in_k(g, k):
        return pltpu.make_async_copy(
            wk.at[cols(k), pl.ds(g * HEAD, HEAD)],
            wall.at[cols(k), pl.ds(512 + 256 * g, HEAD)],
            sem_k.at[g, k],
        )

    def in_v(g, k):
        return pltpu.make_async_copy(
            wv.at[cols(k), pl.ds(g * HEAD, HEAD)],
            wall.at[cols(k), pl.ds(512 + 256 * g + HEAD, HEAD)],
            sem_v.at[g, k],
        )

    def in_q(k):
        return pltpu.make_async_copy(wq.at[cols(k), :], wall.at[cols(k), pl.ds(0, 512)], sem_q.at[k])

    for k in range(kcn):
        in_h(k).start()
        in_k(0, k).start()
        in_v(0, k).start()
    for k in range(kcn):
        in_k(1, k).start()
        in_v(1, k).start()
    for k in range(kcn):
        in_q(k).start()
    do_copies = []
    for g in range(2):
        for t in range(2):
            for m in range(2):
                do_copies.append(
                    pltpu.make_async_copy(
                        dog.at[pl.ds(t * QT, QT), pl.ds((2 * g + m) * HEAD, HEAD)],
                        do.at[g, t, pl.ds(m * QT, QT), :],
                        sem_do.at[4 * g + 2 * t + m],
                    )
                )
    for copy in do_copies:
        copy.start()

    first = ctx * TOK
    lane = lax.broadcasted_iota(jnp.int32, (1, TOK), 1)
    low = jnp.maximum(doc[...].reshape(1, TOK) - first + WINDOW, lane + 1)
    for t in range(2):
        part = low[:, t * QT : (t + 1) * QT] - t * QT
        lo[t] = jnp.concatenate([part, part], axis=1)

    def send_kv(g, far):
        return pltpu.make_async_remote_copy(
            src_ref=kv.at[g, :, pl.ds(2 * TOK, TOK), :],
            dst_ref=kv.at[g, :, pl.ds((1 - far) * TOK, TOK), :],
            send_sem=kv_ss.at[g, far],
            recv_sem=kv_rs.at[g, far],
            device_id=next2 if far else next1,
            device_id_type=MESH,
        )

    for g in range(2):
        acc[:, pl.ds(0, 256)] = jnp.zeros((TOK, 256), F32)

        @pl.loop(0, kcn)
        def _(k):
            if g == 0:
                in_h(k).wait()
            in_k(g, k).wait()
            in_v(g, k).wait()
            acc[:, pl.ds(0, 256)] += jnp.dot(
                h[k], wall[cols(k), pl.ds(512 + 256 * g, 256)], preferred_element_type=F32
            )

        for j in range(2):
            kv[g, j, pl.ds(2 * TOK, TOK), :] = acc[:, pl.ds(j * HEAD, HEAD)].astype(BF16)
        if g == 0:
            pl.semaphore_wait(barrier, 6)
        for far in range(2):
            send_kv(g, far).start()

    acc[...] = jnp.zeros_like(acc)

    @pl.loop(0, kcn)
    def _(k):
        in_q(k).wait()
        acc[...] += jnp.dot(h[k], wall[cols(k), pl.ds(0, 512)], preferred_element_type=F32)

    for g in range(2):
        for t in range(2):
            for m in range(2):
                q[g, t, pl.ds(m * QT, QT), :] = acc[
                    pl.ds(t * QT, QT), pl.ds((2 * g + m) * HEAD, HEAD)
                ].astype(BF16)
    for copy in do_copies:
        copy.wait()

    def same(a, b):
        return 1 - (a + b - 2 * a * b)

    def place(b):
        return pl.multiple_of(128 * (2 * same(lax.rem(b, 2), core) + same(b // 2, zpos)), 128)

    def send_dkv(g, far):
        return pltpu.make_async_remote_copy(
            src_ref=dkv_out.at[g, :, pl.ds((1 - far) * TOK, TOK), :],
            dst_ref=dkv_in.at[far, g],
            send_sem=dkv_ss.at[g, far],
            recv_sem=dkv_rs.at[g, far],
            device_id=prev2 if far else prev1,
            device_id_type=MESH,
        )

    @pl.loop(0, 2)
    def _(g):
        for far in range(2):
            send_kv(g, far).wait_recv()
        for t in range(2):
            lowest = lo[t]
            local = lax.broadcasted_iota(jnp.int32, (CH, 2 * QT), 0)

            def chunk(c):
                return pl.ds(c * CH, CH)

            def keys(j, c):
                return kv[g, j, pl.ds((t + c) * CH, CH), :]

            top = None
            for c in range(5):
                kept = lax.dot_general(keys(0, c), q[g, t], NT, preferred_element_type=F32)
                allowed = local >= lowest - c * CH
                if c == 4:
                    lane2 = lax.broadcasted_iota(jnp.int32, (1, QT), 1)
                    allowed = allowed & (local <= jnp.concatenate([lane2, lane2], axis=1))
                kept = jnp.where(allowed, kept, -jnp.inf)
                s[chunk(c), :] = kept
                here = jnp.max(kept, axis=0, keepdims=True)
                top = here if top is None else jnp.maximum(top, here)

            total, dots = 0.0, 0.0
            for c in range(5):
                grads = lax.dot_general(keys(1, c), do[g, t], NT, preferred_element_type=F32)
                weight = jnp.exp2((s[chunk(c), :] - top) * (SCALE * LOG2E))
                s[chunk(c), :] = weight
                dp[chunk(c), :] = grads
                total = total + jnp.sum(weight, axis=0, keepdims=True)
                dots = dots + jnp.sum(weight * grads, axis=0, keepdims=True)
            inverse = 1.0 / total
            row_dot = dots * inverse

            for c in range(5):
                prob = s[chunk(c), :] * inverse
                low_prob = prob.astype(BF16)
                d_score = (prob * (dp[chunk(c), :] - row_dot)).astype(BF16)
                ds[g, t, chunk(c), :] = d_score
                if t + c < 4:
                    rows = pl.ds((t + c) * CH, CH)
                    d_key = jnp.dot(d_score, q[g, t], preferred_element_type=F32)
                    d_val = jnp.dot(low_prob, do[g, t], preferred_element_type=F32)
                    if t == 1:
                        d_key = d_key + dkv[g, 0, rows, :]
                        d_val = d_val + dkv[g, 1, rows, :]
                    if t == 1 or c == 0:
                        dkv_out[g, 0, rows, :] = (d_key * SCALE).astype(BF16)
                        dkv_out[g, 1, rows, :] = d_val.astype(BF16)
                    else:
                        dkv[g, 0, rows, :] = d_key
                        dkv[g, 1, rows, :] = d_val
                else:
                    pw[g, c - 4 if t == 0 else c - 2] = low_prob

        for far in range(2):
            send_dkv(g, far).start()

    @pl.loop(0, 2)
    def _(g):
        for t in range(2):
            dq = lax.dot_general(
                kv[g, 0, pl.ds(t * QT, KEYS), :], ds[g, t], TN, preferred_element_type=F32
            )
            dq = jnp.transpose(dq * SCALE).astype(BF16)
            for m in range(2):
                feats = pl.ds(pl.multiple_of((2 * g + m) * HEAD, HEAD), HEAD)
                for j in range(2):
                    grad[pl.ds(place(2 * t + j), 128), feats] = dq[
                        m * QT + j * 128 : m * QT + (j + 1) * 128
                    ]

        def own(j, first_low, second_low, third_low, by):
            dkv[g, j, pl.ds(4 * CH, CH), :] = jnp.dot(
                first_low, by[g, 0], preferred_element_type=F32
            ) + jnp.dot(second_low, by[g, 1], preferred_element_type=F32)
            dkv[g, j, pl.ds(5 * CH, CH), :] = jnp.dot(third_low, by[g, 1], preferred_element_type=F32)

        last = pl.ds(4 * CH, CH)
        own(0, ds[g, 0, last, :], ds[g, 1, pl.ds(3 * CH, CH), :], ds[g, 1, last, :], q)
        own(1, pw[g, 0], pw[g, 1], pw[g, 2], do)

    for g in range(2):
        for far in range(2):
            send_dkv(g, far).wait_recv()
        for j in range(2):
            for b in range(4):
                rows = pl.ds(b * 128, 128)
                own = dkv[g, j, pl.ds(2 * TOK + b * 128, 128), :]
                if j == 0:
                    own = own * SCALE
                whole = own + (dkv_in[0, g, j, rows, :].astype(F32) + dkv_in[1, g, j, rows, :].astype(F32))
                grad[pl.ds(place(b), 128), pl.ds(512 + g * 256 + j * HEAD, HEAD)] = whole.astype(BF16)

    def send_r1(c):
        return pltpu.make_async_remote_copy(
            src_ref=rs1_out.at[c], dst_ref=rs1_in.at[c],
            send_sem=r1_ss.at[c], recv_sem=r1_rs.at[c],
            device_id=mate, device_id_type=MESH,
        )

    def out_cols(c):
        return pl.ds(pl.multiple_of(c * nc, nc), nc)

    def send_r2(c):
        return pltpu.make_async_remote_copy(
            src_ref=rs2_out.at[c], dst_ref=rs2_in.at[:, out_cols(c)],
            send_sem=r2_ss.at[c], recv_sem=r2_rs.at[c],
            device_id=across, device_id_type=MESH,
        )

    def out_copy(c):
        return pltpu.make_async_copy(keep.at[c], out.at[:, out_cols(c)], sem_o.at[c])

    def join(c):
        send_r1(c).wait_recv()
        rs2_out[c] = (other[c] + rs1_in[c, pl.ds(0, 128), :].astype(F32)).astype(BF16)
        send_r2(c).start()
        keep[c] = keep[c] + rs1_in[c, pl.ds(128, 128), :].astype(F32)
        out_copy(c).start()

    @pl.loop(0, ncn)
    def _(c):
        part = lax.dot_general(
            grad[...], wall[pl.ds(pl.multiple_of(c * nc, nc), nc), :], NT, preferred_element_type=F32
        )
        rs1_out[c] = part[:256].astype(BF16)
        other[c] = part[256:384]
        keep[c] = part[384:]
        send_r1(c).start()

        @pl.when(c > 0)
        def _():
            join(c - 1)

    join(ncn - 1)

    @pl.loop(0, ncn)
    def _(c):
        out_copy(c).wait()
        send_r1(c).wait_send()
        send_r2(c).wait_send()
        send_r2(c).wait_recv()

    for g in range(2):
        for far in range(2):
            send_kv(g, far).wait_send()
            send_dkv(g, far).wait_send()


def shards(hidden, w_query, key_weight, value_weight, out_gradient, doc_start, *, n_ctx):
    width = hidden.shape[1]
    kcn = 7
    kc = width // kcn
    nc = 256
    ncn = width // nc
    dma = pltpu.SemaphoreType.DMA
    anywhere = pl.BlockSpec(memory_space=pl.ANY)
    own, across = pl.pallas_call(
        functools.partial(kernel, n_ctx, kcn, kc, ncn, nc),
        out_shape=(
            jax.ShapeDtypeStruct((128, width), F32),
            jax.ShapeDtypeStruct((128, width), BF16),
        ),
        in_specs=[anywhere] * 5 + [pl.BlockSpec(memory_space=pltpu.VMEM)],
        out_specs=(anywhere, anywhere),
        scratch_shapes=[
            pltpu.VMEM((kcn, TOK, kc), BF16),
            pltpu.VMEM((width, 1024), BF16),
            pltpu.VMEM((TOK, TOK), F32),
            pltpu.VMEM((2, 2, 3 * TOK, HEAD), BF16),
            pltpu.VMEM((2, 2, 2 * QT, HEAD), BF16),
            pltpu.VMEM((2, 2, 2 * QT, HEAD), BF16),
            pltpu.VMEM((2, 1, 2 * QT), jnp.int32),
            pltpu.VMEM((KEYS, 2 * QT), F32),
            pltpu.VMEM((KEYS, 2 * QT), F32),
            pltpu.VMEM((2, 3, CH, 2 * QT), BF16),
            pltpu.VMEM((2, 2, KEYS, 2 * QT), BF16),
            pltpu.VMEM((2, 2, 3 * TOK, HEAD), F32),
            pltpu.VMEM((2, 2, 2 * TOK, HEAD), BF16),
            pltpu.VMEM((2, 2, 2, TOK, HEAD), BF16),
            pltpu.VMEM((TOK, 1024), BF16),
            pltpu.VMEM((ncn, 256, nc), BF16),
            pltpu.VMEM((ncn, 256, nc), BF16),
            pltpu.VMEM((ncn, 128, nc), BF16),
            pltpu.VMEM((ncn, 128, nc), F32),
            pltpu.VMEM((ncn, 128, nc), F32),
            dma((kcn,)), dma((2, kcn)), dma((2, kcn)), dma((kcn,)), dma((8,)), dma((ncn,)),
            dma((2, 2)), dma((2, 2)), dma((2, 2)), dma((2, 2)),
            dma((ncn,)), dma((ncn,)), dma((ncn,)), dma((ncn,)),
        ],
        compiler_params=pltpu.CompilerParams(
            collective_id=0, has_side_effects=True, vmem_limit_bytes=60 * 1024 * 1024
        ),
    )(hidden, w_query, key_weight, value_weight, out_gradient, doc_start)
    return own + across.astype(F32)


def solution(mesh):
    in_specs = (
        P("ctx", None),
        P(None, "head"),
        P(None, "head"),
        P(None, "head"),
        P("ctx", "head"),
        P("ctx"),
    )
    out_specs = P(("ctx", "head"), None)
    return jax.shard_map(
        functools.partial(shards, n_ctx=mesh.shape["ctx"]),
        mesh=mesh, in_specs=in_specs, out_specs=out_specs, check_vma=False,
    )
```

```python
import functools
import math

import jax
import jax.numpy as jnp
from jax import lax
from jax.experimental import pallas as pl
from jax.experimental.pallas import tpu as pltpu
from jax.sharding import PartitionSpec as P

HEAD = 128
WINDOW = 1024
SCALE = 168.0 ** (-0.5)
LOG2E = math.log2(math.e)
MESH = pl.DeviceIdType.MESH
F32 = jnp.float32
BF16 = jnp.bfloat16

TOK = 512
QT = 256
KEYS = 1280
CH = 256
NT = (((1,), (1,)), ((), ()))
TN = (((0,), (0,)), ((), ()))


def kernel(
    n_ctx, kcn, kc, ncn, nc,
    hid, wq, wk, wv, dog, doc, out, rs2_in,
    h, wall, acc, kv, q, do, lo, s, dp, pw, ds, dkv, dkv_out, dkv_in, grad,
    rs1_out, rs1_in, rs2_out, other, keep,
    sem_h, sem_k, sem_v, sem_q, sem_do, sem_o,
    kv_ss, kv_rs, dkv_ss, dkv_rs, r1_ss, r1_rs, r2_ss, r2_rs,
):
    ctx = lax.axis_index("ctx")
    head = lax.axis_index("head")
    zpos, core = head // 2, lax.rem(head, 2)

    def at_ctx(by):
        return (lax.rem(ctx + by + n_ctx, n_ctx), head)

    next2, prev2 = at_ctx(2), at_ctx(-2)
    odd = lax.rem(ctx, 2)
    pair = (ctx + 1 - 2 * odd, head)
    mate = (ctx, head + 1 - 2 * core)
    across = (ctx, lax.rem(head + 2, 4))

    barrier = pltpu.get_barrier_semaphore()
    for peer in (next2, prev2, pair, mate, across):
        pl.semaphore_signal(barrier, inc=1, device_id=peer, device_id_type=MESH)

    def cols(k):
        return pl.ds(pl.multiple_of(k * kc, 128), kc)

    def in_h(k):
        return pltpu.make_async_copy(hid.at[:, cols(k)], h.at[k], sem_h.at[k])

    def in_k(g, k):
        return pltpu.make_async_copy(
            wk.at[cols(k), pl.ds(g * HEAD, HEAD)],
            wall.at[cols(k), pl.ds(512 + 256 * g, HEAD)],
            sem_k.at[g, k],
        )

    def in_v(g, k):
        return pltpu.make_async_copy(
            wv.at[cols(k), pl.ds(g * HEAD, HEAD)],
            wall.at[cols(k), pl.ds(512 + 256 * g + HEAD, HEAD)],
            sem_v.at[g, k],
        )

    def in_q(k):
        return pltpu.make_async_copy(wq.at[cols(k), :], wall.at[cols(k), pl.ds(0, 512)], sem_q.at[k])

    for k in range(kcn):
        in_h(k).start()
        in_k(0, k).start()
        in_v(0, k).start()
    for k in range(kcn):
        in_k(1, k).start()
        in_v(1, k).start()
    for k in range(kcn):
        in_q(k).start()
    do_copies = []
    for g in range(2):
        for t in range(2):
            for m in range(2):
                do_copies.append(
                    pltpu.make_async_copy(
                        dog.at[pl.ds(t * QT, QT), pl.ds((2 * g + m) * HEAD, HEAD)],
                        do.at[g, t, pl.ds(m * QT, QT), :],
                        sem_do.at[4 * g + 2 * t + m],
                    )
                )
    for copy in do_copies:
        copy.start()

    first = ctx * TOK
    lane = lax.broadcasted_iota(jnp.int32, (1, TOK), 1)
    low = jnp.maximum(doc[...].reshape(1, TOK) - first + WINDOW, lane + 1)
    for t in range(2):
        part = low[:, t * QT : (t + 1) * QT] - t * QT
        lo[t] = jnp.concatenate([part, part], axis=1)

    def send_kv(g, j, far):
        if far:
            source, rows, device = 2 * TOK, 0, next2
        else:
            source, rows, device = pl.multiple_of(2 * TOK * (1 - odd), TOK), TOK, pair
        return pltpu.make_async_remote_copy(
            src_ref=kv.at[g, j, pl.ds(source, TOK), :],
            dst_ref=kv.at[g, j, pl.ds(rows, TOK), :],
            send_sem=kv_ss.at[g, j, far],
            recv_sem=kv_rs.at[g, j, far],
            device_id=device,
            device_id_type=MESH,
        )

    def relay_kv(g, j):
        send_kv(g, j, 1).wait_recv()
        send_kv(g, j, 0).start()

    for g in range(2):
        acc[:, pl.ds(0, 256)] = jnp.zeros((TOK, 256), F32)

        @pl.loop(0, kcn)
        def _(k):
            if g == 0:
                in_h(k).wait()
            in_k(g, k).wait()
            in_v(g, k).wait()
            acc[:, pl.ds(0, 256)] += jnp.dot(
                h[k], wall[cols(k), pl.ds(512 + 256 * g, 256)], preferred_element_type=F32
            )

        for j in range(2):
            kv[g, j, pl.ds(2 * TOK, TOK), :] = acc[:, pl.ds(j * HEAD, HEAD)].astype(BF16)
        if g == 0:
            pl.semaphore_wait(barrier, 5)
        for j in range(2):
            send_kv(g, j, 1).start()

            @pl.when(odd == 0)
            def _():
                send_kv(g, j, 0).start()

    acc[...] = jnp.zeros_like(acc)

    @pl.loop(0, kcn)
    def _(k):
        in_q(k).wait()
        acc[...] += jnp.dot(h[k], wall[cols(k), pl.ds(0, 512)], preferred_element_type=F32)

    for g in range(2):
        for t in range(2):
            for m in range(2):
                q[g, t, pl.ds(m * QT, QT), :] = acc[
                    pl.ds(t * QT, QT), pl.ds((2 * g + m) * HEAD, HEAD)
                ].astype(BF16)
    for copy in do_copies:
        copy.wait()

    def same(a, b):
        return 1 - (a + b - 2 * a * b)

    def place(b):
        return pl.multiple_of(128 * (2 * same(lax.rem(b, 2), core) + same(b // 2, zpos)), 128)

    def send_dkv(g, j, far):
        return pltpu.make_async_remote_copy(
            src_ref=dkv_out.at[g, j, pl.ds((1 - far) * TOK, TOK), :],
            dst_ref=dkv_in.at[far, g, j],
            send_sem=dkv_ss.at[g, j, far],
            recv_sem=dkv_rs.at[g, j, far],
            device_id=prev2 if far else pair,
            device_id_type=MESH,
        )

    def relay_dkv(g, j):
        send_dkv(g, j, 0).wait_recv()
        rows = pl.ds(0, TOK)
        dkv_out[g, j, rows, :] = (
            dkv_out[g, j, rows, :].astype(F32) + dkv_in[0, g, j].astype(F32)
        ).astype(BF16)
        send_dkv(g, j, 1).start()

    @pl.when(odd == 1)
    def _():
        for j in range(2):
            relay_kv(0, j)

    @pl.loop(0, 2)
    def _(g):
        @pl.when(odd == 0)
        def _():
            for j in range(2):
                send_kv(g, j, 1).wait_recv()

        for j in range(2):
            send_kv(g, j, 0).wait_recv()
        for t in range(2):
            lowest = lo[t]
            local = lax.broadcasted_iota(jnp.int32, (CH, 2 * QT), 0)

            def chunk(c):
                return pl.ds(c * CH, CH)

            def keys(j, c):
                return kv[g, j, pl.ds((t + c) * CH, CH), :]

            top = None
            for c in range(5):
                kept = lax.dot_general(keys(0, c), q[g, t], NT, preferred_element_type=F32)
                allowed = local >= lowest - c * CH
                if c == 4:
                    lane2 = lax.broadcasted_iota(jnp.int32, (1, QT), 1)
                    allowed = allowed & (local <= jnp.concatenate([lane2, lane2], axis=1))
                kept = jnp.where(allowed, kept, -jnp.inf)
                s[chunk(c), :] = kept
                here = jnp.max(kept, axis=0, keepdims=True)
                top = here if top is None else jnp.maximum(top, here)

            total, dots = 0.0, 0.0
            for c in range(5):
                grads = lax.dot_general(keys(1, c), do[g, t], NT, preferred_element_type=F32)
                weight = jnp.exp2((s[chunk(c), :] - top) * (SCALE * LOG2E))
                s[chunk(c), :] = weight
                dp[chunk(c), :] = grads
                total = total + jnp.sum(weight, axis=0, keepdims=True)
                dots = dots + jnp.sum(weight * grads, axis=0, keepdims=True)
            inverse = 1.0 / total
            row_dot = dots * inverse

            for c in range(5):
                prob = s[chunk(c), :] * inverse
                low_prob = prob.astype(BF16)
                d_score = (prob * (dp[chunk(c), :] - row_dot)).astype(BF16)
                ds[g, t, chunk(c), :] = d_score
                if t + c < 4:
                    rows = pl.ds((t + c) * CH, CH)
                    d_key = jnp.dot(d_score, q[g, t], preferred_element_type=F32)
                    d_val = jnp.dot(low_prob, do[g, t], preferred_element_type=F32)
                    if t == 1:
                        d_key = d_key + dkv[g, 0, rows, :]
                        d_val = d_val + dkv[g, 1, rows, :]
                    if t == 1 or c == 0:
                        dkv_out[g, 0, rows, :] = (d_key * SCALE).astype(BF16)
                        dkv_out[g, 1, rows, :] = d_val.astype(BF16)
                    else:
                        dkv[g, 0, rows, :] = d_key
                        dkv[g, 1, rows, :] = d_val
                else:
                    pw[g, c - 4 if t == 0 else c - 2] = low_prob

            @pl.when((odd == 1) & (g == 0))
            def _():
                relay_kv(1, t)

        for j in range(2):
            send_dkv(g, j, 0).start()

            @pl.when(odd == 0)
            def _():
                send_dkv(g, j, 1).start()

    @pl.when(odd == 1)
    def _():
        for j in range(2):
            relay_dkv(0, j)

    @pl.loop(0, 2)
    def _(g):
        for t in range(2):
            dq = lax.dot_general(
                kv[g, 0, pl.ds(t * QT, KEYS), :], ds[g, t], TN, preferred_element_type=F32
            )
            dq = jnp.transpose(dq * SCALE).astype(BF16)
            for m in range(2):
                feats = pl.ds(pl.multiple_of((2 * g + m) * HEAD, HEAD), HEAD)
                for j in range(2):
                    grad[pl.ds(place(2 * t + j), 128), feats] = dq[
                        m * QT + j * 128 : m * QT + (j + 1) * 128
                    ]

        def own(j, first_low, second_low, third_low, by):
            dkv[g, j, pl.ds(4 * CH, CH), :] = jnp.dot(
                first_low, by[g, 0], preferred_element_type=F32
            ) + jnp.dot(second_low, by[g, 1], preferred_element_type=F32)
            dkv[g, j, pl.ds(5 * CH, CH), :] = jnp.dot(third_low, by[g, 1], preferred_element_type=F32)

        last = pl.ds(4 * CH, CH)
        own(0, ds[g, 0, last, :], ds[g, 1, pl.ds(3 * CH, CH), :], ds[g, 1, last, :], q)
        own(1, pw[g, 0], pw[g, 1], pw[g, 2], do)

    @pl.when(odd == 1)
    def _():
        for j in range(2):
            relay_dkv(1, j)

    for g in range(2):
        for j in range(2):
            @pl.when(odd == 0)
            def _():
                send_dkv(g, j, 0).wait_recv()

            send_dkv(g, j, 1).wait_recv()
            for b in range(4):
                rows = pl.ds(b * 128, 128)
                own = dkv[g, j, pl.ds(2 * TOK + b * 128, 128), :]
                if j == 0:
                    own = own * SCALE
                near = jnp.where(odd == 0, dkv_in[0, g, j, rows, :].astype(F32), 0.0)
                whole = own + (near + dkv_in[1, g, j, rows, :].astype(F32))
                grad[pl.ds(place(b), 128), pl.ds(512 + g * 256 + j * HEAD, HEAD)] = whole.astype(BF16)

    def send_r1(c):
        return pltpu.make_async_remote_copy(
            src_ref=rs1_out.at[c], dst_ref=rs1_in.at[c],
            send_sem=r1_ss.at[c], recv_sem=r1_rs.at[c],
            device_id=mate, device_id_type=MESH,
        )

    def out_cols(c):
        return pl.ds(pl.multiple_of(c * nc, nc), nc)

    def send_r2(c):
        return pltpu.make_async_remote_copy(
            src_ref=rs2_out.at[c], dst_ref=rs2_in.at[:, out_cols(c)],
            send_sem=r2_ss.at[c], recv_sem=r2_rs.at[c],
            device_id=across, device_id_type=MESH,
        )

    def out_copy(c):
        return pltpu.make_async_copy(keep.at[c], out.at[:, out_cols(c)], sem_o.at[c])

    def join(c):
        send_r1(c).wait_recv()
        rs2_out[c] = (other[c] + rs1_in[c, pl.ds(0, 128), :].astype(F32)).astype(BF16)
        send_r2(c).start()
        keep[c] = keep[c] + rs1_in[c, pl.ds(128, 128), :].astype(F32)
        out_copy(c).start()

    @pl.loop(0, ncn)
    def _(c):
        part = lax.dot_general(
            grad[...], wall[pl.ds(pl.multiple_of(c * nc, nc), nc), :], NT, preferred_element_type=F32
        )
        rs1_out[c] = part[:256].astype(BF16)
        other[c] = part[256:384]
        keep[c] = part[384:]
        send_r1(c).start()

        @pl.when(c > 0)
        def _():
            join(c - 1)

    join(ncn - 1)

    @pl.loop(0, ncn)
    def _(c):
        out_copy(c).wait()
        send_r1(c).wait_send()
        send_r2(c).wait_send()
        send_r2(c).wait_recv()

    for g in range(2):
        for j in range(2):
            for far in range(2):
                send_kv(g, j, far).wait_send()
                send_dkv(g, j, far).wait_send()


def shards(hidden, w_query, key_weight, value_weight, out_gradient, doc_start, *, n_ctx):
    width = hidden.shape[1]
    kcn = 7
    kc = width // kcn
    nc = 256
    ncn = width // nc
    dma = pltpu.SemaphoreType.DMA
    anywhere = pl.BlockSpec(memory_space=pl.ANY)
    own, across = pl.pallas_call(
        functools.partial(kernel, n_ctx, kcn, kc, ncn, nc),
        out_shape=(
            jax.ShapeDtypeStruct((128, width), F32),
            jax.ShapeDtypeStruct((128, width), BF16),
        ),
        in_specs=[anywhere] * 5 + [pl.BlockSpec(memory_space=pltpu.VMEM)],
        out_specs=(anywhere, anywhere),
        scratch_shapes=[
            pltpu.VMEM((kcn, TOK, kc), BF16),
            pltpu.VMEM((width, 1024), BF16),
            pltpu.VMEM((TOK, TOK), F32),
            pltpu.VMEM((2, 2, 3 * TOK, HEAD), BF16),
            pltpu.VMEM((2, 2, 2 * QT, HEAD), BF16),
            pltpu.VMEM((2, 2, 2 * QT, HEAD), BF16),
            pltpu.VMEM((2, 1, 2 * QT), jnp.int32),
            pltpu.VMEM((KEYS, 2 * QT), F32),
            pltpu.VMEM((KEYS, 2 * QT), F32),
            pltpu.VMEM((2, 3, CH, 2 * QT), BF16),
            pltpu.VMEM((2, 2, KEYS, 2 * QT), BF16),
            pltpu.VMEM((2, 2, 3 * TOK, HEAD), F32),
            pltpu.VMEM((2, 2, 2 * TOK, HEAD), BF16),
            pltpu.VMEM((2, 2, 2, TOK, HEAD), BF16),
            pltpu.VMEM((TOK, 1024), BF16),
            pltpu.VMEM((ncn, 256, nc), BF16),
            pltpu.VMEM((ncn, 256, nc), BF16),
            pltpu.VMEM((ncn, 128, nc), BF16),
            pltpu.VMEM((ncn, 128, nc), F32),
            pltpu.VMEM((ncn, 128, nc), F32),
            dma((kcn,)), dma((2, kcn)), dma((2, kcn)), dma((kcn,)), dma((8,)), dma((ncn,)),
            dma((2, 2, 2)), dma((2, 2, 2)), dma((2, 2, 2)), dma((2, 2, 2)),
            dma((ncn,)), dma((ncn,)), dma((ncn,)), dma((ncn,)),
        ],
        compiler_params=pltpu.CompilerParams(
            collective_id=0, has_side_effects=True, vmem_limit_bytes=60 * 1024 * 1024
        ),
    )(hidden, w_query, key_weight, value_weight, out_gradient, doc_start)
    return own + across.astype(F32)


def solution(mesh):
    in_specs = (
        P("ctx", None),
        P(None, "head"),
        P(None, "head"),
        P(None, "head"),
        P("ctx", "head"),
        P("ctx"),
    )
    out_specs = P(("ctx", "head"), None)
    return jax.shard_map(
        functools.partial(shards, n_ctx=mesh.shape["ctx"]),
        mesh=mesh, in_specs=in_specs, out_specs=out_specs, check_vma=False,
    )
```

```python
import functools
import math

import jax
import jax.numpy as jnp
from jax import lax
from jax.experimental import pallas as pl
from jax.experimental.pallas import tpu as pltpu
from jax.sharding import PartitionSpec as P

HEAD = 128
WINDOW = 1024
SCALE = 168.0 ** (-0.5)
LOG2E = math.log2(math.e)
MESH = pl.DeviceIdType.MESH
F32 = jnp.float32
BF16 = jnp.bfloat16

TOK = 512
QT = 256
KEYS = 1280
CH = 256
NT = (((1,), (1,)), ((), ()))
TN = (((0,), (0,)), ((), ()))


def kernel(
    n_ctx, kcn, kc, ncn, nc,
    hid, wq, wk, wv, dog, doc, keep, rs2_in,
    h, wall, acc, kv, q, do, lo, s, dp, pw, ds, dkv, dkv_out, dkv_in, grad,
    rs1_out, rs1_in, rs2_out, other,
    sem_h, sem_k, sem_v, sem_q, sem_do,
    kv_ss, kv_rs, dkv_ss, dkv_rs, r1_ss, r1_rs, r2_ss, r2_rs,
):
    ctx = lax.axis_index("ctx")
    head = lax.axis_index("head")
    zpos, core = head // 2, lax.rem(head, 2)

    def at_ctx(by):
        return (lax.rem(ctx + by + n_ctx, n_ctx), head)

    next2, prev2 = at_ctx(2), at_ctx(-2)
    odd = lax.rem(ctx, 2)
    pair = (ctx + 1 - 2 * odd, head)
    mate = (ctx, head + 1 - 2 * core)
    across = (ctx, lax.rem(head + 2, 4))

    barrier = pltpu.get_barrier_semaphore()
    for peer in (next2, prev2, pair, mate, across):
        pl.semaphore_signal(barrier, inc=1, device_id=peer, device_id_type=MESH)

    def cols(k):
        return pl.ds(pl.multiple_of(k * kc, 128), kc)

    def in_h(k):
        return pltpu.make_async_copy(hid.at[:, cols(k)], h.at[k], sem_h.at[k])

    def in_k(g, k):
        return pltpu.make_async_copy(
            wk.at[cols(k), pl.ds(g * HEAD, HEAD)],
            wall.at[cols(k), pl.ds(512 + 256 * g, HEAD)],
            sem_k.at[g, k],
        )

    def in_v(g, k):
        return pltpu.make_async_copy(
            wv.at[cols(k), pl.ds(g * HEAD, HEAD)],
            wall.at[cols(k), pl.ds(512 + 256 * g + HEAD, HEAD)],
            sem_v.at[g, k],
        )

    def in_q(k):
        return pltpu.make_async_copy(wq.at[cols(k), :], wall.at[cols(k), pl.ds(0, 512)], sem_q.at[k])

    for k in range(kcn):
        in_h(k).start()
        in_k(0, k).start()
        in_v(0, k).start()
    for k in range(kcn):
        in_k(1, k).start()
        in_v(1, k).start()
    for k in range(kcn):
        in_q(k).start()
    do_copies = []
    for g in range(2):
        for t in range(2):
            for m in range(2):
                do_copies.append(
                    pltpu.make_async_copy(
                        dog.at[pl.ds(t * QT, QT), pl.ds((2 * g + m) * HEAD, HEAD)],
                        do.at[g, t, pl.ds(m * QT, QT), :],
                        sem_do.at[4 * g + 2 * t + m],
                    )
                )
    for copy in do_copies:
        copy.start()

    first = ctx * TOK
    lane = lax.broadcasted_iota(jnp.int32, (1, TOK), 1)
    low = jnp.maximum(doc[...].reshape(1, TOK) - first + WINDOW, lane + 1)
    for t in range(2):
        part = low[:, t * QT : (t + 1) * QT] - t * QT
        lo[t] = jnp.concatenate([part, part], axis=1)

    def send_kv(g, j, far):
        if far:
            source, rows, device = 2 * TOK, 0, next2
        else:
            source, rows, device = pl.multiple_of(2 * TOK * (1 - odd), TOK), TOK, pair
        return pltpu.make_async_remote_copy(
            src_ref=kv.at[g, j, pl.ds(source, TOK), :],
            dst_ref=kv.at[g, j, pl.ds(rows, TOK), :],
            send_sem=kv_ss.at[g, j, far],
            recv_sem=kv_rs.at[g, j, far],
            device_id=device,
            device_id_type=MESH,
        )

    def relay_kv(g, j):
        send_kv(g, j, 1).wait_recv()
        send_kv(g, j, 0).start()

    for g in range(2):
        acc[:, pl.ds(0, 256)] = jnp.zeros((TOK, 256), F32)

        @pl.loop(0, kcn)
        def _(k):
            if g == 0:
                in_h(k).wait()
            in_k(g, k).wait()
            in_v(g, k).wait()
            acc[:, pl.ds(0, 256)] += jnp.dot(
                h[k], wall[cols(k), pl.ds(512 + 256 * g, 256)], preferred_element_type=F32
            )

        for j in range(2):
            kv[g, j, pl.ds(2 * TOK, TOK), :] = acc[:, pl.ds(j * HEAD, HEAD)].astype(BF16)
        if g == 0:
            pl.semaphore_wait(barrier, 5)
        for j in range(2):
            send_kv(g, j, 1).start()

            @pl.when(odd == 0)
            def _():
                send_kv(g, j, 0).start()

    acc[...] = jnp.zeros_like(acc)

    @pl.loop(0, kcn)
    def _(k):
        in_q(k).wait()
        acc[...] += jnp.dot(h[k], wall[cols(k), pl.ds(0, 512)], preferred_element_type=F32)

    for g in range(2):
        for t in range(2):
            for m in range(2):
                q[g, t, pl.ds(m * QT, QT), :] = acc[
                    pl.ds(t * QT, QT), pl.ds((2 * g + m) * HEAD, HEAD)
                ].astype(BF16)
    for copy in do_copies:
        copy.wait()

    def same(a, b):
        return 1 - (a + b - 2 * a * b)

    def place(b):
        return pl.multiple_of(128 * (2 * same(lax.rem(b, 2), core) + same(b // 2, zpos)), 128)

    def send_dkv(g, j, far):
        return pltpu.make_async_remote_copy(
            src_ref=dkv_out.at[g, j, pl.ds((1 - far) * TOK, TOK), :],
            dst_ref=dkv_in.at[far, g, j],
            send_sem=dkv_ss.at[g, j, far],
            recv_sem=dkv_rs.at[g, j, far],
            device_id=prev2 if far else pair,
            device_id_type=MESH,
        )

    def relay_dkv(g, j):
        send_dkv(g, j, 0).wait_recv()
        rows = pl.ds(0, TOK)
        dkv_out[g, j, rows, :] = (
            dkv_out[g, j, rows, :].astype(F32) + dkv_in[0, g, j].astype(F32)
        ).astype(BF16)
        send_dkv(g, j, 1).start()

    @pl.when(odd == 1)
    def _():
        for j in range(2):
            relay_kv(0, j)

    @pl.loop(0, 2)
    def _(g):
        @pl.when(odd == 0)
        def _():
            for j in range(2):
                send_kv(g, j, 1).wait_recv()

        for j in range(2):
            send_kv(g, j, 0).wait_recv()
        for t in range(2):
            lowest = lo[t]
            local = lax.broadcasted_iota(jnp.int32, (CH, 2 * QT), 0)

            def chunk(c):
                return pl.ds(c * CH, CH)

            def keys(j, c):
                return kv[g, j, pl.ds((t + c) * CH, CH), :]

            top = None
            for c in range(5):
                kept = lax.dot_general(keys(0, c), q[g, t], NT, preferred_element_type=F32)
                allowed = local >= lowest - c * CH
                if c == 4:
                    lane2 = lax.broadcasted_iota(jnp.int32, (1, QT), 1)
                    allowed = allowed & (local <= jnp.concatenate([lane2, lane2], axis=1))
                kept = jnp.where(allowed, kept, -jnp.inf)
                s[chunk(c), :] = kept
                here = jnp.max(kept, axis=0, keepdims=True)
                top = here if top is None else jnp.maximum(top, here)

            total, dots = 0.0, 0.0
            for c in range(5):
                grads = lax.dot_general(keys(1, c), do[g, t], NT, preferred_element_type=F32)
                weight = jnp.exp2((s[chunk(c), :] - top) * (SCALE * LOG2E))
                s[chunk(c), :] = weight
                dp[chunk(c), :] = grads
                total = total + jnp.sum(weight, axis=0, keepdims=True)
                dots = dots + jnp.sum(weight * grads, axis=0, keepdims=True)
            inverse = 1.0 / total
            row_dot = dots * inverse

            for c in range(5):
                prob = s[chunk(c), :] * inverse
                low_prob = prob.astype(BF16)
                d_score = (prob * (dp[chunk(c), :] - row_dot)).astype(BF16)
                ds[g, t, chunk(c), :] = d_score
                if t + c < 4:
                    rows = pl.ds((t + c) * CH, CH)
                    d_key = jnp.dot(d_score, q[g, t], preferred_element_type=F32)
                    d_val = jnp.dot(low_prob, do[g, t], preferred_element_type=F32)
                    if t == 1:
                        d_key = d_key + dkv[g, 0, rows, :]
                        d_val = d_val + dkv[g, 1, rows, :]
                    if t == 1 or c == 0:
                        dkv_out[g, 0, rows, :] = (d_key * SCALE).astype(BF16)
                        dkv_out[g, 1, rows, :] = d_val.astype(BF16)
                    else:
                        dkv[g, 0, rows, :] = d_key
                        dkv[g, 1, rows, :] = d_val
                else:
                    pw[g, c - 4 if t == 0 else c - 2] = low_prob

            @pl.when((odd == 1) & (g == 0))
            def _():
                relay_kv(1, t)

        for j in range(2):
            send_dkv(g, j, 0).start()

            @pl.when(odd == 0)
            def _():
                send_dkv(g, j, 1).start()

    @pl.when(odd == 1)
    def _():
        for j in range(2):
            relay_dkv(0, j)

    @pl.loop(0, 2)
    def _(g):
        for t in range(2):
            dq = lax.dot_general(
                kv[g, 0, pl.ds(t * QT, KEYS), :], ds[g, t], TN, preferred_element_type=F32
            )
            dq = jnp.transpose(dq * SCALE).astype(BF16)
            for m in range(2):
                feats = pl.ds(pl.multiple_of((2 * g + m) * HEAD, HEAD), HEAD)
                for j in range(2):
                    grad[pl.ds(place(2 * t + j), 128), feats] = dq[
                        m * QT + j * 128 : m * QT + (j + 1) * 128
                    ]

        def own(j, first_low, second_low, third_low, by):
            dkv[g, j, pl.ds(4 * CH, CH), :] = jnp.dot(
                first_low, by[g, 0], preferred_element_type=F32
            ) + jnp.dot(second_low, by[g, 1], preferred_element_type=F32)
            dkv[g, j, pl.ds(5 * CH, CH), :] = jnp.dot(third_low, by[g, 1], preferred_element_type=F32)

        last = pl.ds(4 * CH, CH)
        own(0, ds[g, 0, last, :], ds[g, 1, pl.ds(3 * CH, CH), :], ds[g, 1, last, :], q)
        own(1, pw[g, 0], pw[g, 1], pw[g, 2], do)

    @pl.when(odd == 1)
    def _():
        for j in range(2):
            relay_dkv(1, j)

    for g in range(2):
        for j in range(2):
            @pl.when(odd == 0)
            def _():
                send_dkv(g, j, 0).wait_recv()

            send_dkv(g, j, 1).wait_recv()
            for b in range(4):
                rows = pl.ds(b * 128, 128)
                own = dkv[g, j, pl.ds(2 * TOK + b * 128, 128), :]
                if j == 0:
                    own = own * SCALE
                near = jnp.where(odd == 0, dkv_in[0, g, j, rows, :].astype(F32), 0.0)
                whole = own + (near + dkv_in[1, g, j, rows, :].astype(F32))
                grad[pl.ds(place(b), 128), pl.ds(512 + g * 256 + j * HEAD, HEAD)] = whole.astype(BF16)

    def send_r1(c):
        return pltpu.make_async_remote_copy(
            src_ref=rs1_out.at[c], dst_ref=rs1_in.at[c],
            send_sem=r1_ss.at[c], recv_sem=r1_rs.at[c],
            device_id=mate, device_id_type=MESH,
        )

    def out_cols(c):
        return pl.ds(pl.multiple_of(c * nc, nc), nc)

    def send_r2(c):
        return pltpu.make_async_remote_copy(
            src_ref=rs2_out.at[c], dst_ref=rs2_in.at[:, out_cols(c)],
            send_sem=r2_ss.at[c], recv_sem=r2_rs.at[c],
            device_id=across, device_id_type=MESH,
        )

    def join(c):
        send_r1(c).wait_recv()
        rs2_out[c] = (other[c] + rs1_in[c, pl.ds(0, 128), :].astype(F32)).astype(BF16)
        send_r2(c).start()
        keep[:, out_cols(c)] += rs1_in[c, pl.ds(128, 128), :].astype(F32)

    @pl.loop(0, ncn)
    def _(c):
        part = lax.dot_general(
            grad[...], wall[pl.ds(pl.multiple_of(c * nc, nc), nc), :], NT, preferred_element_type=F32
        )
        rs1_out[c] = part[:256].astype(BF16)
        other[c] = part[256:384]
        keep[:, out_cols(c)] = part[384:]
        send_r1(c).start()

        @pl.when(c > 0)
        def _():
            join(c - 1)

    join(ncn - 1)

    @pl.loop(0, ncn)
    def _(c):
        send_r1(c).wait_send()
        send_r2(c).wait_send()
        send_r2(c).wait_recv()

    for g in range(2):
        for j in range(2):
            for far in range(2):
                send_kv(g, j, far).wait_send()
                send_dkv(g, j, far).wait_send()


def shards(hidden, w_query, key_weight, value_weight, out_gradient, doc_start, *, n_ctx):
    width = hidden.shape[1]
    kcn = 7
    kc = width // kcn
    nc = 256
    ncn = width // nc
    dma = pltpu.SemaphoreType.DMA
    anywhere = pl.BlockSpec(memory_space=pl.ANY)
    own, across = pl.pallas_call(
        functools.partial(kernel, n_ctx, kcn, kc, ncn, nc),
        out_shape=(
            pltpu.VMEM((128, width), F32),
            pltpu.VMEM((128, width), BF16),
        ),
        in_specs=[anywhere] * 5 + [pl.BlockSpec(memory_space=pltpu.VMEM)],
        out_specs=(pl.BlockSpec(memory_space=pltpu.VMEM),) * 2,
        scratch_shapes=[
            pltpu.VMEM((kcn, TOK, kc), BF16),
            pltpu.VMEM((width, 1024), BF16),
            pltpu.VMEM((TOK, TOK), F32),
            pltpu.VMEM((2, 2, 3 * TOK, HEAD), BF16),
            pltpu.VMEM((2, 2, 2 * QT, HEAD), BF16),
            pltpu.VMEM((2, 2, 2 * QT, HEAD), BF16),
            pltpu.VMEM((2, 1, 2 * QT), jnp.int32),
            pltpu.VMEM((KEYS, 2 * QT), F32),
            pltpu.VMEM((KEYS, 2 * QT), F32),
            pltpu.VMEM((2, 3, CH, 2 * QT), BF16),
            pltpu.VMEM((2, 2, KEYS, 2 * QT), BF16),
            pltpu.VMEM((2, 2, 3 * TOK, HEAD), F32),
            pltpu.VMEM((2, 2, 2 * TOK, HEAD), BF16),
            pltpu.VMEM((2, 2, 2, TOK, HEAD), BF16),
            pltpu.VMEM((TOK, 1024), BF16),
            pltpu.VMEM((ncn, 256, nc), BF16),
            pltpu.VMEM((ncn, 256, nc), BF16),
            pltpu.VMEM((ncn, 128, nc), BF16),
            pltpu.VMEM((ncn, 128, nc), F32),
            dma((kcn,)), dma((2, kcn)), dma((2, kcn)), dma((kcn,)), dma((8,)),
            dma((2, 2, 2)), dma((2, 2, 2)), dma((2, 2, 2)), dma((2, 2, 2)),
            dma((ncn,)), dma((ncn,)), dma((ncn,)), dma((ncn,)),
        ],
        compiler_params=pltpu.CompilerParams(
            collective_id=0, has_side_effects=True, vmem_limit_bytes=60 * 1024 * 1024
        ),
    )(hidden, w_query, key_weight, value_weight, out_gradient, doc_start)
    return own + across.astype(F32)


def solution(mesh):
    in_specs = (
        P("ctx", None),
        P(None, "head"),
        P(None, "head"),
        P(None, "head"),
        P("ctx", "head"),
        P("ctx"),
    )
    out_specs = P(("ctx", "head"), None)
    return jax.shard_map(
        functools.partial(shards, n_ctx=mesh.shape["ctx"]),
        mesh=mesh, in_specs=in_specs, out_specs=out_specs, check_vma=False,
    )
```

```python
import functools
import math

import jax
import jax.numpy as jnp
from jax import lax
from jax.experimental import pallas as pl
from jax.experimental.pallas import tpu as pltpu
from jax.sharding import PartitionSpec as P

HEAD = 128
WINDOW = 1024
SCALE = 168.0 ** (-0.5)
LOG2E = math.log2(math.e)
MESH = pl.DeviceIdType.MESH
F32 = jnp.float32
BF16 = jnp.bfloat16

TOK = 512
QT = 256
KEYS = 1280
CH = 256
NT = (((1,), (1,)), ((), ()))
TN = (((0,), (0,)), ((), ()))


def kernel(
    n_ctx, kcn, kc, ncn, nc,
    hid, wq, wk, wv, dog, doc, keep, rs2_in,
    h, wall, acc, kv, q, do, lo, s, dp, pw, ds, dkv, dkv_out, dkv_in, grad,
    rs1_out, rs1_in, rs2_out, other,
    sem_h, sem_k, sem_v, sem_q, sem_do,
    kv_ss, kv_rs, dkv_ss, dkv_rs, r1_ss, r1_rs, r2_ss, r2_rs,
):
    ctx = lax.axis_index("ctx")
    head = lax.axis_index("head")
    zpos, core = head // 2, lax.rem(head, 2)

    def at_ctx(by):
        return (lax.rem(ctx + by + n_ctx, n_ctx), head)

    next2, prev2 = at_ctx(2), at_ctx(-2)
    odd = lax.rem(ctx, 2)
    pair = (ctx + 1 - 2 * odd, head)
    mate = (ctx, head + 1 - 2 * core)
    across = (ctx, lax.rem(head + 2, 4))

    barrier = pltpu.get_barrier_semaphore()
    for peer in (next2, prev2, pair, mate, across):
        pl.semaphore_signal(barrier, inc=1, device_id=peer, device_id_type=MESH)

    def cols(k):
        return pl.ds(pl.multiple_of(k * kc, 128), kc)

    def in_h(k):
        return pltpu.make_async_copy(hid.at[:, cols(k)], h.at[k], sem_h.at[k])

    def in_k(g, k):
        return pltpu.make_async_copy(
            wk.at[cols(k), pl.ds(g * HEAD, HEAD)],
            wall.at[cols(k), pl.ds(512 + 256 * g, HEAD)],
            sem_k.at[g, k],
        )

    def in_v(g, k):
        return pltpu.make_async_copy(
            wv.at[cols(k), pl.ds(g * HEAD, HEAD)],
            wall.at[cols(k), pl.ds(512 + 256 * g + HEAD, HEAD)],
            sem_v.at[g, k],
        )

    def in_q(k):
        return pltpu.make_async_copy(wq.at[cols(k), :], wall.at[cols(k), pl.ds(0, 512)], sem_q.at[k])

    for k in range(kcn):
        in_h(k).start()
        in_k(0, k).start()
        in_v(0, k).start()
    for k in range(kcn):
        in_k(1, k).start()
        in_v(1, k).start()
    for k in range(kcn):
        in_q(k).start()
    do_copies = []
    for g in range(2):
        for t in range(2):
            for m in range(2):
                do_copies.append(
                    pltpu.make_async_copy(
                        dog.at[pl.ds(t * QT, QT), pl.ds((2 * g + m) * HEAD, HEAD)],
                        do.at[g, t, pl.ds(m * QT, QT), :],
                        sem_do.at[4 * g + 2 * t + m],
                    )
                )
    for copy in do_copies:
        copy.start()

    first = ctx * TOK
    lane = lax.broadcasted_iota(jnp.int32, (1, TOK), 1)
    low = jnp.maximum(doc[...].reshape(1, TOK) - first + WINDOW, lane + 1)
    for t in range(2):
        part = low[:, t * QT : (t + 1) * QT] - t * QT
        lo[t] = jnp.concatenate([part, part], axis=1)

    def send_kv(g, j, half, far):
        if far:
            source, rows, device = 2 * TOK, 0, next2
        else:
            source, rows, device = pl.multiple_of(2 * TOK * (1 - odd), TOK), TOK, pair
        return pltpu.make_async_remote_copy(
            src_ref=kv.at[g, j, pl.ds(source + half * QT, QT), :],
            dst_ref=kv.at[g, j, pl.ds(rows + half * QT, QT), :],
            send_sem=kv_ss.at[g, j, half, far],
            recv_sem=kv_rs.at[g, j, half, far],
            device_id=device,
            device_id_type=MESH,
        )

    def relay_kv(g, j):
        for half in range(2):
            send_kv(g, j, half, 1).wait_recv()
            send_kv(g, j, half, 0).start()

    for g in range(2):
        acc[:, pl.ds(0, 256)] = jnp.zeros((TOK, 256), F32)

        @pl.loop(0, kcn)
        def _(k):
            if g == 0:
                in_h(k).wait()
            in_k(g, k).wait()
            in_v(g, k).wait()
            acc[:, pl.ds(0, 256)] += jnp.dot(
                h[k], wall[cols(k), pl.ds(512 + 256 * g, 256)], preferred_element_type=F32
            )

        for j in range(2):
            kv[g, j, pl.ds(2 * TOK, TOK), :] = acc[:, pl.ds(j * HEAD, HEAD)].astype(BF16)
        if g == 0:
            pl.semaphore_wait(barrier, 5)
        for j in range(2):
            for half in range(2):
                send_kv(g, j, half, 1).start()

                @pl.when(odd == 0)
                def _():
                    send_kv(g, j, half, 0).start()

    acc[...] = jnp.zeros_like(acc)

    @pl.loop(0, kcn)
    def _(k):
        in_q(k).wait()
        acc[...] += jnp.dot(h[k], wall[cols(k), pl.ds(0, 512)], preferred_element_type=F32)

    for g in range(2):
        for t in range(2):
            for m in range(2):
                q[g, t, pl.ds(m * QT, QT), :] = acc[
                    pl.ds(t * QT, QT), pl.ds((2 * g + m) * HEAD, HEAD)
                ].astype(BF16)
    for copy in do_copies:
        copy.wait()

    def same(a, b):
        return 1 - (a + b - 2 * a * b)

    def place(b):
        return pl.multiple_of(64 * (2 * same(lax.rem(b, 2), core) + same(b // 2, zpos)), 64)

    def send_dkv(g, j, half, far):
        return pltpu.make_async_remote_copy(
            src_ref=dkv_out.at[g, j, 1 - far, :, half],
            dst_ref=dkv_in.at[far, g, j, :, half],
            send_sem=dkv_ss.at[g, j, half, far],
            recv_sem=dkv_rs.at[g, j, half, far],
            device_id=prev2 if far else pair,
            device_id_type=MESH,
        )

    def relay_dkv(g, j, half):
        send_dkv(g, j, half, 0).wait_recv()
        dkv_out[g, j, 0, :, half] = (
            dkv_out[g, j, 0, :, half].astype(F32) + dkv_in[0, g, j, :, half].astype(F32)
        ).astype(BF16)
        send_dkv(g, j, half, 1).start()

    @pl.when(odd == 1)
    def _():
        for j in range(2):
            relay_kv(0, j)

    @pl.loop(0, 2)
    def _(g):
        @pl.when(odd == 0)
        def _():
            for j in range(2):
                for half in range(2):
                    send_kv(g, j, half, 1).wait_recv()

        for j in range(2):
            for half in range(2):
                send_kv(g, j, half, 0).wait_recv()
        for t in range(2):
            lowest = lo[t]
            local = lax.broadcasted_iota(jnp.int32, (CH, 2 * QT), 0)

            def chunk(c):
                return pl.ds(c * CH, CH)

            def keys(j, c):
                return kv[g, j, pl.ds((t + c) * CH, CH), :]

            top = None
            for c in range(5):
                kept = lax.dot_general(keys(0, c), q[g, t], NT, preferred_element_type=F32)
                allowed = local >= lowest - c * CH
                if c == 4:
                    lane2 = lax.broadcasted_iota(jnp.int32, (1, QT), 1)
                    allowed = allowed & (local <= jnp.concatenate([lane2, lane2], axis=1))
                kept = jnp.where(allowed, kept, -jnp.inf)
                s[chunk(c), :] = kept
                here = jnp.max(kept, axis=0, keepdims=True)
                top = here if top is None else jnp.maximum(top, here)

            total, dots = 0.0, 0.0
            for c in range(5):
                grads = lax.dot_general(keys(1, c), do[g, t], NT, preferred_element_type=F32)
                weight = jnp.exp2((s[chunk(c), :] - top) * (SCALE * LOG2E))
                s[chunk(c), :] = weight
                dp[chunk(c), :] = grads
                total = total + jnp.sum(weight, axis=0, keepdims=True)
                dots = dots + jnp.sum(weight * grads, axis=0, keepdims=True)
            inverse = 1.0 / total
            row_dot = dots * inverse

            for c in range(5):
                prob = s[chunk(c), :] * inverse
                low_prob = prob.astype(BF16)
                d_score = (prob * (dp[chunk(c), :] - row_dot)).astype(BF16)
                ds[g, t, chunk(c), :] = d_score
                if t + c < 4:
                    rows = pl.ds((t + c) * CH, CH)
                    d_key = jnp.dot(d_score, q[g, t], preferred_element_type=F32)
                    d_val = jnp.dot(low_prob, do[g, t], preferred_element_type=F32)
                    if t == 1:
                        d_key = d_key + dkv[g, 0, rows, :]
                        d_val = d_val + dkv[g, 1, rows, :]
                    if t == 1 or c == 0:
                        blocks = pl.ds(2 * ((t + c) % 2), 2)
                        split = (2, 2, 64, HEAD)
                        dkv_out[g, 0, (t + c) // 2, blocks] = (d_key * SCALE).astype(BF16).reshape(split)
                        dkv_out[g, 1, (t + c) // 2, blocks] = d_val.astype(BF16).reshape(split)
                    else:
                        dkv[g, 0, rows, :] = d_key
                        dkv[g, 1, rows, :] = d_val
                else:
                    pw[g, c - 4 if t == 0 else c - 2] = low_prob

            @pl.when((odd == 1) & (g == 0))
            def _():
                relay_kv(1, t)

        for half in range(2):
            for j in range(2):
                send_dkv(g, j, half, 0).start()

                @pl.when(odd == 0)
                def _():
                    send_dkv(g, j, half, 1).start()

    @pl.loop(0, 2)
    def _(g):
        for t in range(2):
            dq = lax.dot_general(
                kv[g, 0, pl.ds(t * QT, KEYS), :], ds[g, t], TN, preferred_element_type=F32
            )
            dq = jnp.transpose(dq * SCALE).astype(BF16)
            for m in range(2):
                feats = pl.ds(pl.multiple_of((2 * g + m) * HEAD, HEAD), HEAD)
                for j in range(2):
                    for half in range(2):
                        start = m * QT + j * 128 + half * 64
                        grad[half, pl.ds(place(2 * t + j), 64), feats] = dq[start : start + 64]

        def own(j, first_low, second_low, third_low, by):
            dkv[g, j, pl.ds(4 * CH, CH), :] = jnp.dot(
                first_low, by[g, 0], preferred_element_type=F32
            ) + jnp.dot(second_low, by[g, 1], preferred_element_type=F32)
            dkv[g, j, pl.ds(5 * CH, CH), :] = jnp.dot(third_low, by[g, 1], preferred_element_type=F32)

        last = pl.ds(4 * CH, CH)
        own(0, ds[g, 0, last, :], ds[g, 1, pl.ds(3 * CH, CH), :], ds[g, 1, last, :], q)
        own(1, pw[g, 0], pw[g, 1], pw[g, 2], do)

    @pl.when(odd == 1)
    def _():
        for g in range(2):
            for half in range(2):
                for j in range(2):
                    relay_dkv(g, j, half)

    def send_r1(half, c):
        return pltpu.make_async_remote_copy(
            src_ref=rs1_out.at[half, c], dst_ref=rs1_in.at[half, c],
            send_sem=r1_ss.at[half, c], recv_sem=r1_rs.at[half, c],
            device_id=mate, device_id_type=MESH,
        )

    def out_cols(c):
        return pl.ds(pl.multiple_of(c * nc, nc), nc)

    def out_rows(half):
        return pl.ds(pl.multiple_of(half * 64, 64), 64)

    def send_r2(half, c):
        return pltpu.make_async_remote_copy(
            src_ref=rs2_out.at[half, c], dst_ref=rs2_in.at[out_rows(half), out_cols(c)],
            send_sem=r2_ss.at[half, c], recv_sem=r2_rs.at[half, c],
            device_id=across, device_id_type=MESH,
        )

    def join(half, c):
        send_r1(half, c).wait_recv()
        rs2_out[half, c] = (other[c] + rs1_in[half, c, pl.ds(0, 64), :].astype(F32)).astype(BF16)
        send_r2(half, c).start()
        keep[out_rows(half), out_cols(c)] += rs1_in[half, c, pl.ds(64, 64), :].astype(F32)

    @pl.loop(0, 2)
    def _(half):
        for g in range(2):
            for j in range(2):
                @pl.when(odd == 0)
                def _():
                    send_dkv(g, j, half, 0).wait_recv()

                send_dkv(g, j, half, 1).wait_recv()
                for b in range(4):
                    own = dkv[g, j, pl.ds(pl.multiple_of(2 * TOK + b * 128 + half * 64, 64), 64), :]
                    if j == 0:
                        own = own * SCALE
                    near = jnp.where(odd == 0, dkv_in[0, g, j, b, half].astype(F32), 0.0)
                    whole = own + (near + dkv_in[1, g, j, b, half].astype(F32))
                    grad[half, pl.ds(place(b), 64), pl.ds(512 + g * 256 + j * HEAD, HEAD)] = whole.astype(BF16)

        @pl.loop(0, ncn)
        def _(c):
            part = lax.dot_general(
                grad[half], wall[out_cols(c), :], NT, preferred_element_type=F32
            )
            rs1_out[half, c] = part[:128].astype(BF16)
            send_r1(half, c).start()

            @pl.when(c > 0)
            def _():
                join(half, c - 1)

            other[c] = part[128:192]
            keep[out_rows(half), out_cols(c)] = part[192:]

        join(half, ncn - 1)

    @pl.loop(0, ncn)
    def _(c):
        for half in range(2):
            send_r1(half, c).wait_send()
            send_r2(half, c).wait_send()
            send_r2(half, c).wait_recv()

    for g in range(2):
        for j in range(2):
            for half in range(2):
                for far in range(2):
                    send_kv(g, j, half, far).wait_send()
                    send_dkv(g, j, half, far).wait_send()


def shards(hidden, w_query, key_weight, value_weight, out_gradient, doc_start, *, n_ctx):
    width = hidden.shape[1]
    kcn = 7
    kc = width // kcn
    nc = 256
    ncn = width // nc
    dma = pltpu.SemaphoreType.DMA
    anywhere = pl.BlockSpec(memory_space=pl.ANY)
    own, across = pl.pallas_call(
        functools.partial(kernel, n_ctx, kcn, kc, ncn, nc),
        out_shape=(
            pltpu.VMEM((128, width), F32),
            pltpu.VMEM((128, width), BF16),
        ),
        in_specs=[anywhere] * 5 + [pl.BlockSpec(memory_space=pltpu.VMEM)],
        out_specs=(pl.BlockSpec(memory_space=pltpu.VMEM),) * 2,
        scratch_shapes=[
            pltpu.VMEM((kcn, TOK, kc), BF16),
            pltpu.VMEM((width, 1024), BF16),
            pltpu.VMEM((TOK, TOK), F32),
            pltpu.VMEM((2, 2, 3 * TOK, HEAD), BF16),
            pltpu.VMEM((2, 2, 2 * QT, HEAD), BF16),
            pltpu.VMEM((2, 2, 2 * QT, HEAD), BF16),
            pltpu.VMEM((2, 1, 2 * QT), jnp.int32),
            pltpu.VMEM((KEYS, 2 * QT), F32),
            pltpu.VMEM((KEYS, 2 * QT), F32),
            pltpu.VMEM((2, 3, CH, 2 * QT), BF16),
            pltpu.VMEM((2, 2, KEYS, 2 * QT), BF16),
            pltpu.VMEM((2, 2, 3 * TOK, HEAD), F32),
            pltpu.VMEM((2, 2, 2, 4, 2, 64, HEAD), BF16),
            pltpu.VMEM((2, 2, 2, 4, 2, 64, HEAD), BF16),
            pltpu.VMEM((2, QT, 1024), BF16),
            pltpu.VMEM((2, ncn, 128, nc), BF16),
            pltpu.VMEM((2, ncn, 128, nc), BF16),
            pltpu.VMEM((2, ncn, 64, nc), BF16),
            pltpu.VMEM((ncn, 64, nc), F32),
            dma((kcn,)), dma((2, kcn)), dma((2, kcn)), dma((kcn,)), dma((8,)),
            dma((2, 2, 2, 2)), dma((2, 2, 2, 2)), dma((2, 2, 2, 2)), dma((2, 2, 2, 2)),
            dma((2, ncn)), dma((2, ncn)), dma((2, ncn)), dma((2, ncn)),
        ],
        compiler_params=pltpu.CompilerParams(
            collective_id=0, has_side_effects=True, vmem_limit_bytes=60 * 1024 * 1024
        ),
    )(hidden, w_query, key_weight, value_weight, out_gradient, doc_start)
    return own + across.astype(F32)


def solution(mesh):
    in_specs = (
        P("ctx", None),
        P(None, "head"),
        P(None, "head"),
        P(None, "head"),
        P("ctx", "head"),
        P("ctx"),
    )
    out_specs = P(("ctx", "head"), None)
    return jax.shard_map(
        functools.partial(shards, n_ctx=mesh.shape["ctx"]),
        mesh=mesh, in_specs=in_specs, out_specs=out_specs, check_vma=False,
    )
```

```python
import functools
import math

import jax
import jax.numpy as jnp
from jax import lax
from jax.experimental import pallas as pl
from jax.experimental.pallas import tpu as pltpu
from jax.sharding import PartitionSpec as P

HEAD = 128
WINDOW = 1024
SCALE = 168.0 ** (-0.5)
LOG2E = math.log2(math.e)
MESH = pl.DeviceIdType.MESH
F32 = jnp.float32
BF16 = jnp.bfloat16

TOK = 512
QT = 256
KEYS = 1280
CH = 256
LAG = 3
NT = (((1,), (1,)), ((), ()))
TN = (((0,), (0,)), ((), ()))


def kernel(
    n_ctx, kcn, kc, ncn, nc,
    hid, wq, wk, wv, dog, doc, keep, rs2_in,
    h, wall, acc, kv, q, do, lo, s, dp, pw, ds, dkv, dkv_out, dkv_in, grad,
    rs1_out, rs1_in, rs2_out, other,
    sem_h, sem_k, sem_v, sem_q, sem_do,
    kv_ss, kv_rs, dkv_ss, dkv_rs, r1_ss, r1_rs, r2_ss, r2_rs,
):
    ctx = lax.axis_index("ctx")
    head = lax.axis_index("head")
    zpos, core = head // 2, lax.rem(head, 2)

    def at_ctx(by):
        return (lax.rem(ctx + by + n_ctx, n_ctx), head)

    next2, prev2 = at_ctx(2), at_ctx(-2)
    odd = lax.rem(ctx, 2)
    pair = (ctx + 1 - 2 * odd, head)
    mate = (ctx, head + 1 - 2 * core)
    across = (ctx, lax.rem(head + 2, 4))

    barrier = pltpu.get_barrier_semaphore()
    for peer in (next2, prev2, pair, mate, across):
        pl.semaphore_signal(barrier, inc=1, device_id=peer, device_id_type=MESH)

    def cols(k):
        return pl.ds(pl.multiple_of(k * kc, 128), kc)

    def in_h(k):
        return pltpu.make_async_copy(hid.at[:, cols(k)], h.at[k], sem_h.at[k])

    def in_k(g, k):
        return pltpu.make_async_copy(
            wk.at[cols(k), pl.ds(g * HEAD, HEAD)],
            wall.at[cols(k), pl.ds(512 + 256 * g, HEAD)],
            sem_k.at[g, k],
        )

    def in_v(g, k):
        return pltpu.make_async_copy(
            wv.at[cols(k), pl.ds(g * HEAD, HEAD)],
            wall.at[cols(k), pl.ds(512 + 256 * g + HEAD, HEAD)],
            sem_v.at[g, k],
        )

    def in_q(k):
        return pltpu.make_async_copy(wq.at[cols(k), :], wall.at[cols(k), pl.ds(0, 512)], sem_q.at[k])

    for k in range(kcn):
        in_h(k).start()
        in_k(0, k).start()
        in_v(0, k).start()
    for k in range(kcn):
        in_k(1, k).start()
        in_v(1, k).start()
    for k in range(kcn):
        in_q(k).start()
    do_copies = []
    for g in range(2):
        for t in range(2):
            for m in range(2):
                do_copies.append(
                    pltpu.make_async_copy(
                        dog.at[pl.ds(t * QT, QT), pl.ds((2 * g + m) * HEAD, HEAD)],
                        do.at[g, t, pl.ds(m * QT, QT), :],
                        sem_do.at[4 * g + 2 * t + m],
                    )
                )
    for copy in do_copies:
        copy.start()

    first = ctx * TOK
    lane = lax.broadcasted_iota(jnp.int32, (1, TOK), 1)
    low = jnp.maximum(doc[...].reshape(1, TOK) - first + WINDOW, lane + 1)
    for t in range(2):
        part = low[:, t * QT : (t + 1) * QT] - t * QT
        lo[t] = jnp.concatenate([part, part], axis=1)

    def send_kv(g, j, half, far):
        if far:
            source, rows, device = 2 * TOK, 0, next2
        else:
            source, rows, device = pl.multiple_of(2 * TOK * (1 - odd), TOK), TOK, pair
        return pltpu.make_async_remote_copy(
            src_ref=kv.at[g, j, pl.ds(source + half * QT, QT), :],
            dst_ref=kv.at[g, j, pl.ds(rows + half * QT, QT), :],
            send_sem=kv_ss.at[g, j, half, far],
            recv_sem=kv_rs.at[g, j, half, far],
            device_id=device,
            device_id_type=MESH,
        )

    def relay_kv(g, j):
        for half in range(2):
            send_kv(g, j, half, 1).wait_recv()
            send_kv(g, j, half, 0).start()

    for g in range(2):
        acc[:, pl.ds(0, 256)] = jnp.zeros((TOK, 256), F32)

        @pl.loop(0, kcn)
        def _(k):
            if g == 0:
                in_h(k).wait()
            in_k(g, k).wait()
            in_v(g, k).wait()
            acc[:, pl.ds(0, 256)] += jnp.dot(
                h[k], wall[cols(k), pl.ds(512 + 256 * g, 256)], preferred_element_type=F32
            )

        for j in range(2):
            kv[g, j, pl.ds(2 * TOK, TOK), :] = acc[:, pl.ds(j * HEAD, HEAD)].astype(BF16)
        if g == 0:
            pl.semaphore_wait(barrier, 5)
        for j in range(2):
            for half in range(2):
                send_kv(g, j, half, 1).start()

                @pl.when(odd == 0)
                def _():
                    send_kv(g, j, half, 0).start()

    acc[...] = jnp.zeros_like(acc)

    @pl.loop(0, kcn)
    def _(k):
        in_q(k).wait()
        acc[...] += jnp.dot(h[k], wall[cols(k), pl.ds(0, 512)], preferred_element_type=F32)

    for g in range(2):
        for t in range(2):
            for m in range(2):
                q[g, t, pl.ds(m * QT, QT), :] = acc[
                    pl.ds(t * QT, QT), pl.ds((2 * g + m) * HEAD, HEAD)
                ].astype(BF16)
    for copy in do_copies:
        copy.wait()

    def same(a, b):
        return 1 - (a + b - 2 * a * b)

    def place(b):
        return pl.multiple_of(64 * (2 * same(lax.rem(b, 2), core) + same(b // 2, zpos)), 64)

    def send_dkv(g, j, half, far):
        return pltpu.make_async_remote_copy(
            src_ref=dkv_out.at[g, j, 1 - far, :, half],
            dst_ref=dkv_in.at[far, g, j, :, half],
            send_sem=dkv_ss.at[g, j, half, far],
            recv_sem=dkv_rs.at[g, j, half, far],
            device_id=prev2 if far else pair,
            device_id_type=MESH,
        )

    def relay_dkv(g, j, half):
        send_dkv(g, j, half, 0).wait_recv()
        dkv_out[g, j, 0, :, half] = (
            dkv_out[g, j, 0, :, half].astype(F32) + dkv_in[0, g, j, :, half].astype(F32)
        ).astype(BF16)
        send_dkv(g, j, half, 1).start()

    @pl.when(odd == 1)
    def _():
        for j in range(2):
            relay_kv(0, j)

    @pl.loop(0, 2)
    def _(g):
        @pl.when(odd == 0)
        def _():
            for j in range(2):
                for half in range(2):
                    send_kv(g, j, half, 1).wait_recv()

        for j in range(2):
            for half in range(2):
                send_kv(g, j, half, 0).wait_recv()
        for t in range(2):
            lowest = lo[t]
            local = lax.broadcasted_iota(jnp.int32, (CH, 2 * QT), 0)

            def chunk(c):
                return pl.ds(c * CH, CH)

            def keys(j, c):
                return kv[g, j, pl.ds((t + c) * CH, CH), :]

            top = None
            for c in range(5):
                kept = lax.dot_general(keys(0, c), q[g, t], NT, preferred_element_type=F32)
                allowed = local >= lowest - c * CH
                if c == 4:
                    lane2 = lax.broadcasted_iota(jnp.int32, (1, QT), 1)
                    allowed = allowed & (local <= jnp.concatenate([lane2, lane2], axis=1))
                kept = jnp.where(allowed, kept, -jnp.inf)
                s[chunk(c), :] = kept
                here = jnp.max(kept, axis=0, keepdims=True)
                top = here if top is None else jnp.maximum(top, here)

            total, dots = 0.0, 0.0
            for c in range(5):
                grads = lax.dot_general(keys(1, c), do[g, t], NT, preferred_element_type=F32)
                weight = jnp.exp2((s[chunk(c), :] - top) * (SCALE * LOG2E))
                s[chunk(c), :] = weight
                dp[chunk(c), :] = grads
                total = total + jnp.sum(weight, axis=0, keepdims=True)
                dots = dots + jnp.sum(weight * grads, axis=0, keepdims=True)
            inverse = 1.0 / total
            row_dot = dots * inverse

            for c in range(5):
                prob = s[chunk(c), :] * inverse
                low_prob = prob.astype(BF16)
                d_score = (prob * (dp[chunk(c), :] - row_dot)).astype(BF16)
                ds[g, t, chunk(c), :] = d_score
                if t + c < 4:
                    rows = pl.ds((t + c) * CH, CH)
                    d_key = jnp.dot(d_score, q[g, t], preferred_element_type=F32)
                    d_val = jnp.dot(low_prob, do[g, t], preferred_element_type=F32)
                    if t == 1:
                        d_key = d_key + dkv[g, 0, rows, :]
                        d_val = d_val + dkv[g, 1, rows, :]
                    if t == 1 or c == 0:
                        blocks = pl.ds(2 * ((t + c) % 2), 2)
                        split = (2, 2, 64, HEAD)
                        dkv_out[g, 0, (t + c) // 2, blocks] = (d_key * SCALE).astype(BF16).reshape(split)
                        dkv_out[g, 1, (t + c) // 2, blocks] = d_val.astype(BF16).reshape(split)
                    else:
                        dkv[g, 0, rows, :] = d_key
                        dkv[g, 1, rows, :] = d_val
                else:
                    pw[g, c - 4 if t == 0 else c - 2] = low_prob

            @pl.when((odd == 1) & (g == 0))
            def _():
                relay_kv(1, t)

        for half in range(2):
            for j in range(2):
                send_dkv(g, j, half, 0).start()

                @pl.when(odd == 0)
                def _():
                    send_dkv(g, j, half, 1).start()

    @pl.loop(0, 2)
    def _(g):
        for t in range(2):
            dq = lax.dot_general(
                kv[g, 0, pl.ds(t * QT, KEYS), :], ds[g, t], TN, preferred_element_type=F32
            )
            dq = jnp.transpose(dq * SCALE).astype(BF16)
            for m in range(2):
                feats = pl.ds(pl.multiple_of((2 * g + m) * HEAD, HEAD), HEAD)
                for j in range(2):
                    for half in range(2):
                        start = m * QT + j * 128 + half * 64
                        grad[half, pl.ds(place(2 * t + j), 64), feats] = dq[start : start + 64]

        def own(j, first_low, second_low, third_low, by):
            dkv[g, j, pl.ds(4 * CH, CH), :] = jnp.dot(
                first_low, by[g, 0], preferred_element_type=F32
            ) + jnp.dot(second_low, by[g, 1], preferred_element_type=F32)
            dkv[g, j, pl.ds(5 * CH, CH), :] = jnp.dot(third_low, by[g, 1], preferred_element_type=F32)

        last = pl.ds(4 * CH, CH)
        own(0, ds[g, 0, last, :], ds[g, 1, pl.ds(3 * CH, CH), :], ds[g, 1, last, :], q)
        own(1, pw[g, 0], pw[g, 1], pw[g, 2], do)

    @pl.when(odd == 1)
    def _():
        for g in range(2):
            for half in range(2):
                for j in range(2):
                    relay_dkv(g, j, half)

    def send_r1(half, c):
        return pltpu.make_async_remote_copy(
            src_ref=rs1_out.at[half, c], dst_ref=rs1_in.at[half, c],
            send_sem=r1_ss.at[half, c], recv_sem=r1_rs.at[half, c],
            device_id=mate, device_id_type=MESH,
        )

    def out_cols(c):
        return pl.ds(pl.multiple_of(c * nc, nc), nc)

    def out_rows(half):
        return pl.ds(pl.multiple_of(half * 64, 64), 64)

    def send_r2(half, c):
        return pltpu.make_async_remote_copy(
            src_ref=rs2_out.at[half, c], dst_ref=rs2_in.at[out_rows(half), out_cols(c)],
            send_sem=r2_ss.at[half, c], recv_sem=r2_rs.at[half, c],
            device_id=across, device_id_type=MESH,
        )

    def join(half, c):
        send_r1(half, c).wait_recv()
        rs2_out[half, c] = (other[c] + rs1_in[half, c, pl.ds(0, 64), :].astype(F32)).astype(BF16)
        send_r2(half, c).start()
        keep[out_rows(half), out_cols(c)] += rs1_in[half, c, pl.ds(64, 64), :].astype(F32)

    @pl.loop(0, 2)
    def _(half):
        for g in range(2):
            for j in range(2):
                @pl.when(odd == 0)
                def _():
                    send_dkv(g, j, half, 0).wait_recv()

                send_dkv(g, j, half, 1).wait_recv()
                for b in range(4):
                    own = dkv[g, j, pl.ds(pl.multiple_of(2 * TOK + b * 128 + half * 64, 64), 64), :]
                    if j == 0:
                        own = own * SCALE
                    near = jnp.where(odd == 0, dkv_in[0, g, j, b, half].astype(F32), 0.0)
                    whole = own + (near + dkv_in[1, g, j, b, half].astype(F32))
                    grad[half, pl.ds(place(b), 64), pl.ds(512 + g * 256 + j * HEAD, HEAD)] = whole.astype(BF16)

        @pl.loop(0, ncn)
        def _(c):
            part = lax.dot_general(
                grad[half], wall[out_cols(c), :], NT, preferred_element_type=F32
            )
            rs1_out[half, c] = part[:128].astype(BF16)
            send_r1(half, c).start()

            @pl.when(c >= LAG)
            def _():
                join(half, c - LAG)

            other[c] = part[128:192]
            keep[out_rows(half), out_cols(c)] = part[192:]

        for c in range(ncn - LAG, ncn):
            join(half, c)

    @pl.loop(0, ncn)
    def _(c):
        for half in range(2):
            send_r1(half, c).wait_send()
            send_r2(half, c).wait_send()
            send_r2(half, c).wait_recv()

    for g in range(2):
        for j in range(2):
            for half in range(2):
                for far in range(2):
                    send_kv(g, j, half, far).wait_send()
                    send_dkv(g, j, half, far).wait_send()


def shards(hidden, w_query, key_weight, value_weight, out_gradient, doc_start, *, n_ctx):
    width = hidden.shape[1]
    kcn = 7
    kc = width // kcn
    nc = 256
    ncn = width // nc
    dma = pltpu.SemaphoreType.DMA
    anywhere = pl.BlockSpec(memory_space=pl.ANY)
    own, across = pl.pallas_call(
        functools.partial(kernel, n_ctx, kcn, kc, ncn, nc),
        out_shape=(
            pltpu.VMEM((128, width), F32),
            pltpu.VMEM((128, width), BF16),
        ),
        in_specs=[anywhere] * 5 + [pl.BlockSpec(memory_space=pltpu.VMEM)],
        out_specs=(pl.BlockSpec(memory_space=pltpu.VMEM),) * 2,
        scratch_shapes=[
            pltpu.VMEM((kcn, TOK, kc), BF16),
            pltpu.VMEM((width, 1024), BF16),
            pltpu.VMEM((TOK, TOK), F32),
            pltpu.VMEM((2, 2, 3 * TOK, HEAD), BF16),
            pltpu.VMEM((2, 2, 2 * QT, HEAD), BF16),
            pltpu.VMEM((2, 2, 2 * QT, HEAD), BF16),
            pltpu.VMEM((2, 1, 2 * QT), jnp.int32),
            pltpu.VMEM((KEYS, 2 * QT), F32),
            pltpu.VMEM((KEYS, 2 * QT), F32),
            pltpu.VMEM((2, 3, CH, 2 * QT), BF16),
            pltpu.VMEM((2, 2, KEYS, 2 * QT), BF16),
            pltpu.VMEM((2, 2, 3 * TOK, HEAD), F32),
            pltpu.VMEM((2, 2, 2, 4, 2, 64, HEAD), BF16),
            pltpu.VMEM((2, 2, 2, 4, 2, 64, HEAD), BF16),
            pltpu.VMEM((2, QT, 1024), BF16),
            pltpu.VMEM((2, ncn, 128, nc), BF16),
            pltpu.VMEM((2, ncn, 128, nc), BF16),
            pltpu.VMEM((2, ncn, 64, nc), BF16),
            pltpu.VMEM((ncn, 64, nc), F32),
            dma((kcn,)), dma((2, kcn)), dma((2, kcn)), dma((kcn,)), dma((8,)),
            dma((2, 2, 2, 2)), dma((2, 2, 2, 2)), dma((2, 2, 2, 2)), dma((2, 2, 2, 2)),
            dma((2, ncn)), dma((2, ncn)), dma((2, ncn)), dma((2, ncn)),
        ],
        compiler_params=pltpu.CompilerParams(
            collective_id=0, has_side_effects=True, vmem_limit_bytes=60 * 1024 * 1024
        ),
    )(hidden, w_query, key_weight, value_weight, out_gradient, doc_start)
    return own + across.astype(F32)


def solution(mesh):
    in_specs = (
        P("ctx", None),
        P(None, "head"),
        P(None, "head"),
        P(None, "head"),
        P("ctx", "head"),
        P("ctx"),
    )
    out_specs = P(("ctx", "head"), None)
    return jax.shard_map(
        functools.partial(shards, n_ctx=mesh.shape["ctx"]),
        mesh=mesh, in_specs=in_specs, out_specs=out_specs, check_vma=False,
    )
```

```python
import functools
import math

import jax
import jax.numpy as jnp
from jax import lax
from jax.experimental import pallas as pl
from jax.experimental.pallas import tpu as pltpu
from jax.sharding import PartitionSpec as P

HEAD = 128
WINDOW = 1024
SCALE = 168.0 ** (-0.5)
LOG2E = math.log2(math.e)
MESH = pl.DeviceIdType.MESH
F32 = jnp.float32
BF16 = jnp.bfloat16

TOK = 512
QT = 256
KEYS = 1280
CH = 256
LAG = 2
NT = (((1,), (1,)), ((), ()))
TN = (((0,), (0,)), ((), ()))


def kernel(
    n_ctx, kcn, kc, ncn, nc,
    hid, wq, wk, wv, dog, doc, keep, rs2_in,
    h, wall, acc, kv, q, do, lo, s, dp, pw, ds, dkv, dkv_out, dkv_in, grad,
    rs1_out, rs1_in, rs2_out, other,
    sem_h, sem_k, sem_v, sem_q, sem_do,
    kv_ss, kv_rs, dkv_ss, dkv_rs, r1_ss, r1_rs, r2_ss, r2_rs,
):
    ctx = lax.axis_index("ctx")
    head = lax.axis_index("head")
    zpos, core = head // 2, lax.rem(head, 2)

    def at_ctx(by):
        return (lax.rem(ctx + by + n_ctx, n_ctx), head)

    next2, prev2 = at_ctx(2), at_ctx(-2)
    odd = lax.rem(ctx, 2)
    pair = (ctx + 1 - 2 * odd, head)
    mate = (ctx, head + 1 - 2 * core)
    across = (ctx, lax.rem(head + 2, 4))

    barrier = pltpu.get_barrier_semaphore()
    for peer in (next2, prev2, pair, mate, across):
        pl.semaphore_signal(barrier, inc=1, device_id=peer, device_id_type=MESH)

    def cols(k):
        return pl.ds(pl.multiple_of(k * kc, 128), kc)

    def in_h(k):
        return pltpu.make_async_copy(hid.at[:, cols(k)], h.at[k], sem_h.at[k])

    def in_k(g, k):
        return pltpu.make_async_copy(
            wk.at[cols(k), pl.ds(g * HEAD, HEAD)],
            wall.at[cols(k), pl.ds(512 + 256 * g, HEAD)],
            sem_k.at[g, k],
        )

    def in_v(g, k):
        return pltpu.make_async_copy(
            wv.at[cols(k), pl.ds(g * HEAD, HEAD)],
            wall.at[cols(k), pl.ds(512 + 256 * g + HEAD, HEAD)],
            sem_v.at[g, k],
        )

    def in_q(k):
        return pltpu.make_async_copy(wq.at[cols(k), :], wall.at[cols(k), pl.ds(0, 512)], sem_q.at[k])

    for k in range(kcn):
        in_h(k).start()
        in_k(0, k).start()
        in_v(0, k).start()
    for k in range(kcn):
        in_k(1, k).start()
        in_v(1, k).start()
    for k in range(kcn):
        in_q(k).start()
    do_copies = []
    for g in range(2):
        for t in range(2):
            for m in range(2):
                do_copies.append(
                    pltpu.make_async_copy(
                        dog.at[pl.ds(t * QT, QT), pl.ds((2 * g + m) * HEAD, HEAD)],
                        do.at[g, t, pl.ds(m * QT, QT), :],
                        sem_do.at[4 * g + 2 * t + m],
                    )
                )
    for copy in do_copies:
        copy.start()

    first = ctx * TOK
    lane = lax.broadcasted_iota(jnp.int32, (1, TOK), 1)
    low = jnp.maximum(doc[...].reshape(1, TOK) - first + WINDOW, lane + 1)
    for t in range(2):
        part = low[:, t * QT : (t + 1) * QT] - t * QT
        lo[t] = jnp.concatenate([part, part], axis=1)

    def send_kv(g, j, half, far):
        if far:
            source, rows, device = 2 * TOK, 0, next2
        else:
            source, rows, device = pl.multiple_of(2 * TOK * (1 - odd), TOK), TOK, pair
        return pltpu.make_async_remote_copy(
            src_ref=kv.at[g, j, pl.ds(source + half * QT, QT), :],
            dst_ref=kv.at[g, j, pl.ds(rows + half * QT, QT), :],
            send_sem=kv_ss.at[g, j, half, far],
            recv_sem=kv_rs.at[g, j, half, far],
            device_id=device,
            device_id_type=MESH,
        )

    def relay_kv(g, j):
        for half in range(2):
            send_kv(g, j, half, 1).wait_recv()
            send_kv(g, j, half, 0).start()

    for g in range(2):
        acc[:, pl.ds(0, 256)] = jnp.zeros((TOK, 256), F32)

        @pl.loop(0, kcn)
        def _(k):
            if g == 0:
                in_h(k).wait()
            in_k(g, k).wait()
            in_v(g, k).wait()
            acc[:, pl.ds(0, 256)] += jnp.dot(
                h[k], wall[cols(k), pl.ds(512 + 256 * g, 256)], preferred_element_type=F32
            )

        for j in range(2):
            kv[g, j, pl.ds(2 * TOK, TOK), :] = acc[:, pl.ds(j * HEAD, HEAD)].astype(BF16)
        if g == 0:
            pl.semaphore_wait(barrier, 5)
        for j in range(2):
            for half in range(2):
                send_kv(g, j, half, 1).start()

                @pl.when(odd == 0)
                def _():
                    send_kv(g, j, half, 0).start()

    acc[...] = jnp.zeros_like(acc)

    @pl.loop(0, kcn)
    def _(k):
        in_q(k).wait()
        acc[...] += jnp.dot(h[k], wall[cols(k), pl.ds(0, 512)], preferred_element_type=F32)

    for g in range(2):
        for t in range(2):
            for m in range(2):
                q[g, t, pl.ds(m * QT, QT), :] = acc[
                    pl.ds(t * QT, QT), pl.ds((2 * g + m) * HEAD, HEAD)
                ].astype(BF16)
    for copy in do_copies:
        copy.wait()

    def same(a, b):
        return 1 - (a + b - 2 * a * b)

    def place(b):
        return pl.multiple_of(64 * (2 * same(lax.rem(b, 2), core) + same(b // 2, zpos)), 64)

    def send_dkv(g, j, half, far):
        return pltpu.make_async_remote_copy(
            src_ref=dkv_out.at[g, j, 1 - far, :, half],
            dst_ref=dkv_in.at[far, g, j, :, half],
            send_sem=dkv_ss.at[g, j, half, far],
            recv_sem=dkv_rs.at[g, j, half, far],
            device_id=prev2 if far else pair,
            device_id_type=MESH,
        )

    def relay_dkv(g, j, half):
        send_dkv(g, j, half, 0).wait_recv()
        dkv_out[g, j, 0, :, half] = (
            dkv_out[g, j, 0, :, half].astype(F32) + dkv_in[0, g, j, :, half].astype(F32)
        ).astype(BF16)
        send_dkv(g, j, half, 1).start()

    @pl.when(odd == 1)
    def _():
        for j in range(2):
            relay_kv(0, j)

    def wait_far(g, j):
        @pl.when(odd == 0)
        def _():
            for half in range(2):
                send_kv(g, j, half, 1).wait_recv()

    def wait_near(g, j):
        for half in range(2):
            send_kv(g, j, half, 0).wait_recv()

    def chunk(c):
        return pl.ds(c * CH, CH)

    near_of = ((2, 3), (1, 2))
    far_of = ((0, 1), (0,))
    own_of = ((4,), (3, 4))

    @pl.loop(0, 2)
    def _(g):
        local = lax.broadcasted_iota(jnp.int32, (CH, 2 * QT), 0)
        lane2 = lax.broadcasted_iota(jnp.int32, (1, QT), 1)
        edge = jnp.concatenate([lane2, lane2], axis=1)
        top = [None, None]
        total, dots = [0.0, 0.0], [0.0, 0.0]

        def keys(j, t, c):
            return kv[g, j, pl.ds((t + c) * CH, CH), :]

        def score(t, c):
            kept = lax.dot_general(keys(0, t, c), q[g, t], NT, preferred_element_type=F32)
            allowed = local >= lo[t] - c * CH
            if c == 4:
                allowed = allowed & (local <= edge)
            kept = jnp.where(allowed, kept, -jnp.inf)
            s[t, chunk(c), :] = kept
            here = jnp.max(kept, axis=0, keepdims=True)
            top[t] = here if top[t] is None else jnp.maximum(top[t], here)

        def weigh(t, c):
            grads = lax.dot_general(keys(1, t, c), do[g, t], NT, preferred_element_type=F32)
            weight = jnp.exp2((s[t, chunk(c), :] - top[t]) * (SCALE * LOG2E))
            s[t, chunk(c), :] = weight
            dp[t, chunk(c), :] = grads
            total[t] = total[t] + jnp.sum(weight, axis=0, keepdims=True)
            dots[t] = dots[t] + jnp.sum(weight * grads, axis=0, keepdims=True)

        def back(t, c, inverse, row_dot):
            prob = s[t, chunk(c), :] * inverse
            low_prob = prob.astype(BF16)
            d_score = (prob * (dp[t, chunk(c), :] - row_dot)).astype(BF16)
            ds[g, t, chunk(c), :] = d_score
            if t + c >= 4:
                pw[g, c - 4 if t == 0 else c - 2] = low_prob
                return
            rows = pl.ds((t + c) * CH, CH)
            d_key = jnp.dot(d_score, q[g, t], preferred_element_type=F32)
            d_val = jnp.dot(low_prob, do[g, t], preferred_element_type=F32)
            if t == 1:
                d_key = d_key + dkv[g, 0, rows, :]
                d_val = d_val + dkv[g, 1, rows, :]
            if t == 1 or c == 0:
                blocks = pl.ds(2 * ((t + c) % 2), 2)
                split = (2, 2, 64, HEAD)
                dkv_out[g, 0, (t + c) // 2, blocks] = (d_key * SCALE).astype(BF16).reshape(split)
                dkv_out[g, 1, (t + c) // 2, blocks] = d_val.astype(BF16).reshape(split)
            else:
                dkv[g, 0, rows, :] = d_key
                dkv[g, 1, rows, :] = d_val

        for t in range(2):
            for c in own_of[t]:
                score(t, c)
        wait_far(g, 0)
        for t in range(2):
            for c in far_of[t]:
                score(t, c)
        wait_near(g, 0)
        for t in range(2):
            for c in near_of[t]:
                score(t, c)
        wait_far(g, 1)
        for t in range(2):
            for c in own_of[t] + far_of[t]:
                weigh(t, c)

        @pl.when((odd == 1) & (g == 0))
        def _():
            relay_kv(1, 0)

        wait_near(g, 1)
        for t in range(2):
            for c in near_of[t]:
                weigh(t, c)
        inverse = [1.0 / total[t] for t in range(2)]
        row_dot = [dots[t] * inverse[t] for t in range(2)]
        for t in range(2):
            for c in near_of[t]:
                back(t, c, inverse[t], row_dot[t])
        back(0, 1, inverse[0], row_dot[0])
        for half in range(2):
            for j in range(2):
                send_dkv(g, j, half, 0).start()
        back(0, 0, inverse[0], row_dot[0])
        back(1, 0, inverse[1], row_dot[1])

        @pl.when(odd == 0)
        def _():
            for half in range(2):
                for j in range(2):
                    send_dkv(g, j, half, 1).start()

        @pl.when((odd == 1) & (g == 0))
        def _():
            relay_kv(1, 1)

        for t in range(2):
            for c in own_of[t]:
                back(t, c, inverse[t], row_dot[t])

    @pl.loop(0, 2)
    def _(g):
        for t in range(2):
            dq = lax.dot_general(
                kv[g, 0, pl.ds(t * QT, KEYS), :], ds[g, t], TN, preferred_element_type=F32
            )
            dq = jnp.transpose(dq * SCALE).astype(BF16)
            for m in range(2):
                feats = pl.ds(pl.multiple_of((2 * g + m) * HEAD, HEAD), HEAD)
                for j in range(2):
                    for half in range(2):
                        start = m * QT + j * 128 + half * 64
                        grad[half, pl.ds(place(2 * t + j), 64), feats] = dq[start : start + 64]

        def own(j, first_low, second_low, third_low, by):
            dkv[g, j, pl.ds(4 * CH, CH), :] = jnp.dot(
                first_low, by[g, 0], preferred_element_type=F32
            ) + jnp.dot(second_low, by[g, 1], preferred_element_type=F32)
            dkv[g, j, pl.ds(5 * CH, CH), :] = jnp.dot(third_low, by[g, 1], preferred_element_type=F32)

        last = pl.ds(4 * CH, CH)
        own(0, ds[g, 0, last, :], ds[g, 1, pl.ds(3 * CH, CH), :], ds[g, 1, last, :], q)
        own(1, pw[g, 0], pw[g, 1], pw[g, 2], do)

    @pl.when(odd == 1)
    def _():
        for g in range(2):
            for half in range(2):
                for j in range(2):
                    relay_dkv(g, j, half)

    def send_r1(half, c):
        return pltpu.make_async_remote_copy(
            src_ref=rs1_out.at[half, c], dst_ref=rs1_in.at[half, c],
            send_sem=r1_ss.at[half, c], recv_sem=r1_rs.at[half, c],
            device_id=mate, device_id_type=MESH,
        )

    def out_cols(c):
        return pl.ds(pl.multiple_of(c * nc, nc), nc)

    def out_rows(half):
        return pl.ds(pl.multiple_of(half * 64, 64), 64)

    def send_r2(half, c):
        return pltpu.make_async_remote_copy(
            src_ref=rs2_out.at[half, c], dst_ref=rs2_in.at[out_rows(half), out_cols(c)],
            send_sem=r2_ss.at[half, c], recv_sem=r2_rs.at[half, c],
            device_id=across, device_id_type=MESH,
        )

    def join(half, c):
        send_r1(half, c).wait_recv()
        rs2_out[half, c] = (other[c] + rs1_in[half, c, pl.ds(0, 64), :].astype(F32)).astype(BF16)
        send_r2(half, c).start()
        keep[out_rows(half), out_cols(c)] += rs1_in[half, c, pl.ds(64, 64), :].astype(F32)

    @pl.loop(0, 2)
    def _(half):
        for g in range(2):
            for j in range(2):
                @pl.when(odd == 0)
                def _():
                    send_dkv(g, j, half, 0).wait_recv()

                send_dkv(g, j, half, 1).wait_recv()
                for b in range(4):
                    own = dkv[g, j, pl.ds(pl.multiple_of(2 * TOK + b * 128 + half * 64, 64), 64), :]
                    if j == 0:
                        own = own * SCALE
                    near = jnp.where(odd == 0, dkv_in[0, g, j, b, half].astype(F32), 0.0)
                    whole = own + (near + dkv_in[1, g, j, b, half].astype(F32))
                    grad[half, pl.ds(place(b), 64), pl.ds(512 + g * 256 + j * HEAD, HEAD)] = whole.astype(BF16)

        @pl.loop(0, ncn)
        def _(c):
            part = lax.dot_general(
                grad[half], wall[out_cols(c), :], NT, preferred_element_type=F32
            )
            rs1_out[half, c] = part[:128].astype(BF16)
            send_r1(half, c).start()

            @pl.when(c >= LAG)
            def _():
                join(half, c - LAG)

            other[c] = part[128:192]
            keep[out_rows(half), out_cols(c)] = part[192:]

        for c in range(ncn - LAG, ncn):
            join(half, c)

    @pl.loop(0, ncn)
    def _(c):
        for half in range(2):
            send_r1(half, c).wait_send()
            send_r2(half, c).wait_send()
            send_r2(half, c).wait_recv()

    for g in range(2):
        for j in range(2):
            for half in range(2):
                for far in range(2):
                    send_kv(g, j, half, far).wait_send()
                    send_dkv(g, j, half, far).wait_send()


def shards(hidden, w_query, key_weight, value_weight, out_gradient, doc_start, *, n_ctx):
    width = hidden.shape[1]
    kcn = 7
    kc = width // kcn
    nc = 256
    ncn = width // nc
    dma = pltpu.SemaphoreType.DMA
    anywhere = pl.BlockSpec(memory_space=pl.ANY)
    own, across = pl.pallas_call(
        functools.partial(kernel, n_ctx, kcn, kc, ncn, nc),
        out_shape=(
            pltpu.VMEM((128, width), F32),
            pltpu.VMEM((128, width), BF16),
        ),
        in_specs=[anywhere] * 5 + [pl.BlockSpec(memory_space=pltpu.VMEM)],
        out_specs=(pl.BlockSpec(memory_space=pltpu.VMEM),) * 2,
        scratch_shapes=[
            pltpu.VMEM((kcn, TOK, kc), BF16),
            pltpu.VMEM((width, 1024), BF16),
            pltpu.VMEM((TOK, TOK), F32),
            pltpu.VMEM((2, 2, 3 * TOK, HEAD), BF16),
            pltpu.VMEM((2, 2, 2 * QT, HEAD), BF16),
            pltpu.VMEM((2, 2, 2 * QT, HEAD), BF16),
            pltpu.VMEM((2, 1, 2 * QT), jnp.int32),
            pltpu.VMEM((2, KEYS, 2 * QT), F32),
            pltpu.VMEM((2, KEYS, 2 * QT), F32),
            pltpu.VMEM((2, 3, CH, 2 * QT), BF16),
            pltpu.VMEM((2, 2, KEYS, 2 * QT), BF16),
            pltpu.VMEM((2, 2, 3 * TOK, HEAD), F32),
            pltpu.VMEM((2, 2, 2, 4, 2, 64, HEAD), BF16),
            pltpu.VMEM((2, 2, 2, 4, 2, 64, HEAD), BF16),
            pltpu.VMEM((2, QT, 1024), BF16),
            pltpu.VMEM((2, ncn, 128, nc), BF16),
            pltpu.VMEM((2, ncn, 128, nc), BF16),
            pltpu.VMEM((2, ncn, 64, nc), BF16),
            pltpu.VMEM((ncn, 64, nc), F32),
            dma((kcn,)), dma((2, kcn)), dma((2, kcn)), dma((kcn,)), dma((8,)),
            dma((2, 2, 2, 2)), dma((2, 2, 2, 2)), dma((2, 2, 2, 2)), dma((2, 2, 2, 2)),
            dma((2, ncn)), dma((2, ncn)), dma((2, ncn)), dma((2, ncn)),
        ],
        compiler_params=pltpu.CompilerParams(
            collective_id=0, has_side_effects=True, vmem_limit_bytes=60 * 1024 * 1024
        ),
    )(hidden, w_query, key_weight, value_weight, out_gradient, doc_start)
    return own + across.astype(F32)


def solution(mesh):
    in_specs = (
        P("ctx", None),
        P(None, "head"),
        P(None, "head"),
        P(None, "head"),
        P("ctx", "head"),
        P("ctx"),
    )
    out_specs = P(("ctx", "head"), None)
    return jax.shard_map(
        functools.partial(shards, n_ctx=mesh.shape["ctx"]),
        mesh=mesh, in_specs=in_specs, out_specs=out_specs, check_vma=False,
    )
```

```python
import functools
import math

import jax
import jax.numpy as jnp
from jax import lax
from jax.experimental import pallas as pl
from jax.experimental.pallas import tpu as pltpu
from jax.sharding import PartitionSpec as P

HEAD = 128
WINDOW = 1024
SCALE = 168.0 ** (-0.5)
LOG2E = math.log2(math.e)
MESH = pl.DeviceIdType.MESH
F32 = jnp.float32
BF16 = jnp.bfloat16

TOK = 512
QT = 256
KEYS = 1280
CH = 256
LAG = 2
NT = (((1,), (1,)), ((), ()))
TN = (((0,), (0,)), ((), ()))


def kernel(
    n_ctx, kcn, kc, ncn, nc,
    hid, wq, wk, wv, dog, doc, keep, rs2_in,
    h, wall, acc, kv, q, do, lo, s, dp, pw, ds, dkv, dkv_out, dkv_in, grad,
    rs1_out, rs1_in, rs2_out, other,
    sem_h, sem_k, sem_v, sem_q, sem_do,
    kv_ss, kv_rs, dkv_ss, dkv_rs, r1_ss, r1_rs, r2_ss, r2_rs,
):
    ctx = lax.axis_index("ctx")
    head = lax.axis_index("head")
    zpos, core = head // 2, lax.rem(head, 2)

    def at_ctx(by):
        return (lax.rem(ctx + by + n_ctx, n_ctx), head)

    next2, prev2 = at_ctx(2), at_ctx(-2)
    odd = lax.rem(ctx, 2)
    pair = (ctx + 1 - 2 * odd, head)
    mate = (ctx, head + 1 - 2 * core)
    across = (ctx, lax.rem(head + 2, 4))

    barrier = pltpu.get_barrier_semaphore()
    for peer in (next2, prev2, pair, mate, across):
        pl.semaphore_signal(barrier, inc=1, device_id=peer, device_id_type=MESH)

    def cols(k):
        return pl.ds(pl.multiple_of(k * kc, 128), kc)

    def in_h(k):
        return pltpu.make_async_copy(hid.at[:, cols(k)], h.at[k], sem_h.at[k])

    def in_k(g, k):
        return pltpu.make_async_copy(
            wk.at[cols(k), pl.ds(g * HEAD, HEAD)],
            wall.at[cols(k), pl.ds(512 + 256 * g, HEAD)],
            sem_k.at[g, k],
        )

    def in_v(g, k):
        return pltpu.make_async_copy(
            wv.at[cols(k), pl.ds(g * HEAD, HEAD)],
            wall.at[cols(k), pl.ds(512 + 256 * g + HEAD, HEAD)],
            sem_v.at[g, k],
        )

    def in_q(k):
        return pltpu.make_async_copy(wq.at[cols(k), :], wall.at[cols(k), pl.ds(0, 512)], sem_q.at[k])

    for k in range(kcn):
        in_h(k).start()
        in_k(0, k).start()
        in_v(0, k).start()
    for k in range(kcn):
        in_k(1, k).start()
        in_v(1, k).start()
    for k in range(kcn):
        in_q(k).start()
    do_copies = []
    for g in range(2):
        for t in range(2):
            for m in range(2):
                do_copies.append(
                    pltpu.make_async_copy(
                        dog.at[pl.ds(t * QT, QT), pl.ds((2 * g + m) * HEAD, HEAD)],
                        do.at[g, t, pl.ds(m * QT, QT), :],
                        sem_do.at[4 * g + 2 * t + m],
                    )
                )
    for copy in do_copies:
        copy.start()

    first = ctx * TOK
    lane = lax.broadcasted_iota(jnp.int32, (1, TOK), 1)
    low = jnp.maximum(doc[...].reshape(1, TOK) - first + WINDOW, lane + 1)
    for t in range(2):
        part = low[:, t * QT : (t + 1) * QT] - t * QT
        lo[t] = jnp.concatenate([part, part], axis=1)

    def send_kv(g, j, half, far):
        if far:
            source, rows, device = 2 * TOK, 0, next2
        else:
            source, rows, device = pl.multiple_of(2 * TOK * (1 - odd), TOK), TOK, pair
        return pltpu.make_async_remote_copy(
            src_ref=kv.at[g, j, pl.ds(source + half * QT, QT), :],
            dst_ref=kv.at[g, j, pl.ds(rows + half * QT, QT), :],
            send_sem=kv_ss.at[g, j, half, far],
            recv_sem=kv_rs.at[g, j, half, far],
            device_id=device,
            device_id_type=MESH,
        )

    def relay_kv(g, j):
        for half in range(2):
            send_kv(g, j, half, 1).wait_recv()
            send_kv(g, j, half, 0).start()

    for g in range(2):
        acc[:, pl.ds(0, 256)] = jnp.zeros((TOK, 256), F32)

        @pl.loop(0, kcn)
        def _(k):
            if g == 0:
                in_h(k).wait()
            in_k(g, k).wait()
            in_v(g, k).wait()
            acc[:, pl.ds(0, 256)] += jnp.dot(
                h[k], wall[cols(k), pl.ds(512 + 256 * g, 256)], preferred_element_type=F32
            )

        for j in range(2):
            kv[g, j, pl.ds(2 * TOK, TOK), :] = acc[:, pl.ds(j * HEAD, HEAD)].astype(BF16)
        if g == 0:
            pl.semaphore_wait(barrier, 5)
        for j in range(2):
            for half in range(2):
                send_kv(g, j, half, 1).start()

                @pl.when(odd == 0)
                def _():
                    send_kv(g, j, half, 0).start()

    acc[...] = jnp.zeros_like(acc)

    @pl.loop(0, kcn)
    def _(k):
        in_q(k).wait()
        acc[...] += jnp.dot(h[k], wall[cols(k), pl.ds(0, 512)], preferred_element_type=F32)

    for g in range(2):
        for t in range(2):
            for m in range(2):
                q[g, t, pl.ds(m * QT, QT), :] = acc[
                    pl.ds(t * QT, QT), pl.ds((2 * g + m) * HEAD, HEAD)
                ].astype(BF16)
    for copy in do_copies:
        copy.wait()

    def same(a, b):
        return 1 - (a + b - 2 * a * b)

    def place(b):
        return pl.multiple_of(64 * (2 * same(lax.rem(b, 2), core) + same(b // 2, zpos)), 64)

    def send_dkv(g, j, half, far):
        return pltpu.make_async_remote_copy(
            src_ref=dkv_out.at[g, j, 1 - far, :, half],
            dst_ref=dkv_in.at[far, g, j, :, half],
            send_sem=dkv_ss.at[g, j, half, far],
            recv_sem=dkv_rs.at[g, j, half, far],
            device_id=prev2 if far else pair,
            device_id_type=MESH,
        )

    def relay_dkv(g, j, half):
        send_dkv(g, j, half, 0).wait_recv()
        dkv_out[g, j, 0, :, half] = (
            dkv_out[g, j, 0, :, half].astype(F32) + dkv_in[0, g, j, :, half].astype(F32)
        ).astype(BF16)
        send_dkv(g, j, half, 1).start()

    @pl.when(odd == 1)
    def _():
        for j in range(2):
            relay_kv(0, j)

    def wait_far(g, j):
        @pl.when(odd == 0)
        def _():
            for half in range(2):
                send_kv(g, j, half, 1).wait_recv()

    def wait_near(g, j):
        for half in range(2):
            send_kv(g, j, half, 0).wait_recv()

    def chunk(c):
        return pl.ds(c * CH, CH)

    near_of = ((2, 3), (1, 2))
    far_of = ((0, 1), (0,))
    own_of = ((4,), (3, 4))

    @pl.loop(0, 2)
    def _(g):
        local = lax.broadcasted_iota(jnp.int32, (CH, 2 * QT), 0)
        lane2 = lax.broadcasted_iota(jnp.int32, (1, QT), 1)
        edge = jnp.concatenate([lane2, lane2], axis=1)
        top = [None, None]
        total, dots = [0.0, 0.0], [0.0, 0.0]

        def keys(j, t, c):
            return kv[g, j, pl.ds((t + c) * CH, CH), :]

        def score(t, c):
            kept = lax.dot_general(keys(0, t, c), q[g, t], NT, preferred_element_type=F32)
            allowed = local >= lo[t] - c * CH
            if c == 4:
                allowed = allowed & (local <= edge)
            kept = jnp.where(allowed, kept, -jnp.inf)
            s[t, chunk(c), :] = kept
            here = jnp.max(kept, axis=0, keepdims=True)
            top[t] = here if top[t] is None else jnp.maximum(top[t], here)

        def weigh(t, c):
            grads = lax.dot_general(keys(1, t, c), do[g, t], NT, preferred_element_type=F32)
            weight = jnp.exp2((s[t, chunk(c), :] - top[t]) * (SCALE * LOG2E))
            s[t, chunk(c), :] = weight
            dp[t, chunk(c), :] = grads
            total[t] = total[t] + jnp.sum(weight, axis=0, keepdims=True)
            dots[t] = dots[t] + jnp.sum(weight * grads, axis=0, keepdims=True)

        def back(t, c, inverse, row_dot):
            prob = s[t, chunk(c), :] * inverse
            low_prob = prob.astype(BF16)
            d_score = (prob * (dp[t, chunk(c), :] - row_dot)).astype(BF16)
            ds[g, t, chunk(c), :] = d_score
            if t + c >= 4:
                pw[g, c - 4 if t == 0 else c - 2] = low_prob
                return
            rows = pl.ds((t + c) * CH, CH)
            d_key = jnp.dot(d_score, q[g, t], preferred_element_type=F32)
            d_val = jnp.dot(low_prob, do[g, t], preferred_element_type=F32)
            if t == 1:
                d_key = d_key + dkv[g, 0, rows, :]
                d_val = d_val + dkv[g, 1, rows, :]
            if t == 1 or c == 0:
                blocks = pl.ds(2 * ((t + c) % 2), 2)
                split = (2, 2, 64, HEAD)
                dkv_out[g, 0, (t + c) // 2, blocks] = (d_key * SCALE).astype(BF16).reshape(split)
                dkv_out[g, 1, (t + c) // 2, blocks] = d_val.astype(BF16).reshape(split)
            else:
                dkv[g, 0, rows, :] = d_key
                dkv[g, 1, rows, :] = d_val

        for t in range(2):
            for c in own_of[t]:
                score(t, c)
        wait_far(g, 0)
        for t in range(2):
            for c in far_of[t]:
                score(t, c)
        wait_near(g, 0)
        for t in range(2):
            for c in near_of[t]:
                score(t, c)
        wait_far(g, 1)
        for t in range(2):
            for c in own_of[t] + far_of[t]:
                weigh(t, c)

        @pl.when((odd == 1) & (g == 0))
        def _():
            relay_kv(1, 0)

        wait_near(g, 1)
        for t in range(2):
            for c in near_of[t]:
                weigh(t, c)
        inverse = [1.0 / total[t] for t in range(2)]
        row_dot = [dots[t] * inverse[t] for t in range(2)]
        for t in range(2):
            for c in near_of[t]:
                back(t, c, inverse[t], row_dot[t])
        back(0, 1, inverse[0], row_dot[0])
        back(0, 0, inverse[0], row_dot[0])
        back(1, 0, inverse[1], row_dot[1])
        for half in range(2):
            for j in range(2):
                send_dkv(g, j, half, 0).start()

                @pl.when(odd == 0)
                def _():
                    send_dkv(g, j, half, 1).start()

        @pl.when((odd == 1) & (g == 0))
        def _():
            relay_kv(1, 1)

        for t in range(2):
            for c in own_of[t]:
                back(t, c, inverse[t], row_dot[t])

    @pl.loop(0, 2)
    def _(g):
        for t in range(2):
            dq = lax.dot_general(
                kv[g, 0, pl.ds(t * QT, KEYS), :], ds[g, t], TN, preferred_element_type=F32
            )
            dq = jnp.transpose(dq * SCALE).astype(BF16)
            for m in range(2):
                feats = pl.ds(pl.multiple_of((2 * g + m) * HEAD, HEAD), HEAD)
                for j in range(2):
                    for half in range(2):
                        start = m * QT + j * 128 + half * 64
                        grad[half, pl.ds(place(2 * t + j), 64), feats] = dq[start : start + 64]

        def own(j, first_low, second_low, third_low, by):
            dkv[g, j, pl.ds(4 * CH, CH), :] = jnp.dot(
                first_low, by[g, 0], preferred_element_type=F32
            ) + jnp.dot(second_low, by[g, 1], preferred_element_type=F32)
            dkv[g, j, pl.ds(5 * CH, CH), :] = jnp.dot(third_low, by[g, 1], preferred_element_type=F32)

        last = pl.ds(4 * CH, CH)
        own(0, ds[g, 0, last, :], ds[g, 1, pl.ds(3 * CH, CH), :], ds[g, 1, last, :], q)
        own(1, pw[g, 0], pw[g, 1], pw[g, 2], do)

    @pl.when(odd == 1)
    def _():
        for g in range(2):
            for half in range(2):
                for j in range(2):
                    relay_dkv(g, j, half)

    def send_r1(half, c):
        return pltpu.make_async_remote_copy(
            src_ref=rs1_out.at[half, c], dst_ref=rs1_in.at[half, c],
            send_sem=r1_ss.at[half, c], recv_sem=r1_rs.at[half, c],
            device_id=mate, device_id_type=MESH,
        )

    def out_cols(c):
        return pl.ds(pl.multiple_of(c * nc, nc), nc)

    def out_rows(half):
        return pl.ds(pl.multiple_of(half * 64, 64), 64)

    def send_r2(half, c):
        return pltpu.make_async_remote_copy(
            src_ref=rs2_out.at[half, c], dst_ref=rs2_in.at[out_rows(half), out_cols(c)],
            send_sem=r2_ss.at[half, c], recv_sem=r2_rs.at[half, c],
            device_id=across, device_id_type=MESH,
        )

    def join(half, c):
        send_r1(half, c).wait_recv()
        rs2_out[half, c] = (other[c] + rs1_in[half, c, pl.ds(0, 64), :].astype(F32)).astype(BF16)
        send_r2(half, c).start()
        keep[out_rows(half), out_cols(c)] += rs1_in[half, c, pl.ds(64, 64), :].astype(F32)

    @pl.loop(0, 2)
    def _(half):
        for g in range(2):
            for j in range(2):
                @pl.when(odd == 0)
                def _():
                    send_dkv(g, j, half, 0).wait_recv()

                send_dkv(g, j, half, 1).wait_recv()
                for b in range(4):
                    own = dkv[g, j, pl.ds(pl.multiple_of(2 * TOK + b * 128 + half * 64, 64), 64), :]
                    if j == 0:
                        own = own * SCALE
                    near = jnp.where(odd == 0, dkv_in[0, g, j, b, half].astype(F32), 0.0)
                    whole = own + (near + dkv_in[1, g, j, b, half].astype(F32))
                    grad[half, pl.ds(place(b), 64), pl.ds(512 + g * 256 + j * HEAD, HEAD)] = whole.astype(BF16)

        @pl.loop(0, ncn)
        def _(c):
            part = lax.dot_general(
                grad[half], wall[out_cols(c), :], NT, preferred_element_type=F32
            )
            rs1_out[half, c] = part[:128].astype(BF16)
            send_r1(half, c).start()

            @pl.when(c >= LAG)
            def _():
                join(half, c - LAG)

            other[c] = part[128:192]
            keep[out_rows(half), out_cols(c)] = part[192:]

        for c in range(ncn - LAG, ncn):
            join(half, c)

    @pl.loop(0, ncn)
    def _(c):
        for half in range(2):
            send_r1(half, c).wait_send()
            send_r2(half, c).wait_send()
            send_r2(half, c).wait_recv()

    for g in range(2):
        for j in range(2):
            for half in range(2):
                for far in range(2):
                    send_kv(g, j, half, far).wait_send()
                    send_dkv(g, j, half, far).wait_send()


def shards(hidden, w_query, key_weight, value_weight, out_gradient, doc_start, *, n_ctx):
    width = hidden.shape[1]
    kcn = 7
    kc = width // kcn
    nc = 256
    ncn = width // nc
    dma = pltpu.SemaphoreType.DMA
    anywhere = pl.BlockSpec(memory_space=pl.ANY)
    own, across = pl.pallas_call(
        functools.partial(kernel, n_ctx, kcn, kc, ncn, nc),
        out_shape=(
            pltpu.VMEM((128, width), F32),
            pltpu.VMEM((128, width), BF16),
        ),
        in_specs=[anywhere] * 5 + [pl.BlockSpec(memory_space=pltpu.VMEM)],
        out_specs=(pl.BlockSpec(memory_space=pltpu.VMEM),) * 2,
        scratch_shapes=[
            pltpu.VMEM((kcn, TOK, kc), BF16),
            pltpu.VMEM((width, 1024), BF16),
            pltpu.VMEM((TOK, TOK), F32),
            pltpu.VMEM((2, 2, 3 * TOK, HEAD), BF16),
            pltpu.VMEM((2, 2, 2 * QT, HEAD), BF16),
            pltpu.VMEM((2, 2, 2 * QT, HEAD), BF16),
            pltpu.VMEM((2, 1, 2 * QT), jnp.int32),
            pltpu.VMEM((2, KEYS, 2 * QT), F32),
            pltpu.VMEM((2, KEYS, 2 * QT), F32),
            pltpu.VMEM((2, 3, CH, 2 * QT), BF16),
            pltpu.VMEM((2, 2, KEYS, 2 * QT), BF16),
            pltpu.VMEM((2, 2, 3 * TOK, HEAD), F32),
            pltpu.VMEM((2, 2, 2, 4, 2, 64, HEAD), BF16),
            pltpu.VMEM((2, 2, 2, 4, 2, 64, HEAD), BF16),
            pltpu.VMEM((2, QT, 1024), BF16),
            pltpu.VMEM((2, ncn, 128, nc), BF16),
            pltpu.VMEM((2, ncn, 128, nc), BF16),
            pltpu.VMEM((2, ncn, 64, nc), BF16),
            pltpu.VMEM((ncn, 64, nc), F32),
            dma((kcn,)), dma((2, kcn)), dma((2, kcn)), dma((kcn,)), dma((8,)),
            dma((2, 2, 2, 2)), dma((2, 2, 2, 2)), dma((2, 2, 2, 2)), dma((2, 2, 2, 2)),
            dma((2, ncn)), dma((2, ncn)), dma((2, ncn)), dma((2, ncn)),
        ],
        compiler_params=pltpu.CompilerParams(
            collective_id=0, has_side_effects=True, vmem_limit_bytes=60 * 1024 * 1024
        ),
    )(hidden, w_query, key_weight, value_weight, out_gradient, doc_start)
    return own + across.astype(F32)


def solution(mesh):
    in_specs = (
        P("ctx", None),
        P(None, "head"),
        P(None, "head"),
        P(None, "head"),
        P("ctx", "head"),
        P("ctx"),
    )
    out_specs = P(("ctx", "head"), None)
    return jax.shard_map(
        functools.partial(shards, n_ctx=mesh.shape["ctx"]),
        mesh=mesh, in_specs=in_specs, out_specs=out_specs, check_vma=False,
    )
```

```python
import functools
import math

import jax
import jax.numpy as jnp
from jax import lax
from jax.experimental import pallas as pl
from jax.experimental.pallas import tpu as pltpu
from jax.sharding import PartitionSpec as P

HEAD = 128
WINDOW = 1024
SCALE = 168.0 ** (-0.5)
LOG2E = math.log2(math.e)
MESH = pl.DeviceIdType.MESH
F32 = jnp.float32
BF16 = jnp.bfloat16

TOK = 512
QT = 256
KEYS = 1280
CH = 256
NT = (((1,), (1,)), ((), ()))
TN = (((0,), (0,)), ((), ()))


def kernel(
    n_ctx, kcn, kc, ncn, nc,
    hid, wq, wk, wv, dog, doc, keep, rs2_in,
    h, wall, acc, kv, q, do, lo, s, dp, pw, ds, dkv, dkv_out, dkv_in, grad,
    rs1_out, rs1_in, rs2_out, other,
    sem_h, sem_k, sem_v, sem_q, sem_do,
    kv_ss, kv_rs, dkv_ss, dkv_rs, r1_ss, r1_rs, r2_ss, r2_rs,
):
    ctx = lax.axis_index("ctx")
    head = lax.axis_index("head")
    zpos, core = head // 2, lax.rem(head, 2)

    def at_ctx(by):
        return (lax.rem(ctx + by + n_ctx, n_ctx), head)

    next2, prev2 = at_ctx(2), at_ctx(-2)
    odd = lax.rem(ctx, 2)
    pair = (ctx + 1 - 2 * odd, head)
    mate = (ctx, head + 1 - 2 * core)
    across = (ctx, lax.rem(head + 2, 4))

    barrier = pltpu.get_barrier_semaphore()
    for peer in (next2, prev2, pair, mate, across):
        pl.semaphore_signal(barrier, inc=1, device_id=peer, device_id_type=MESH)

    def cols(k):
        return pl.ds(pl.multiple_of(k * kc, 128), kc)

    def in_h(k):
        return pltpu.make_async_copy(hid.at[:, cols(k)], h.at[k], sem_h.at[k])

    def in_k(g, k):
        return pltpu.make_async_copy(
            wk.at[cols(k), pl.ds(g * HEAD, HEAD)],
            wall.at[cols(k), pl.ds(512 + 256 * g, HEAD)],
            sem_k.at[g, k],
        )

    def in_v(g, k):
        return pltpu.make_async_copy(
            wv.at[cols(k), pl.ds(g * HEAD, HEAD)],
            wall.at[cols(k), pl.ds(512 + 256 * g + HEAD, HEAD)],
            sem_v.at[g, k],
        )

    def in_q(k):
        return pltpu.make_async_copy(wq.at[cols(k), :], wall.at[cols(k), pl.ds(0, 512)], sem_q.at[k])

    for k in range(kcn):
        in_h(k).start()
        in_k(0, k).start()
        in_v(0, k).start()
    for k in range(kcn):
        in_k(1, k).start()
        in_v(1, k).start()
    for k in range(kcn):
        in_q(k).start()
    do_copies = []
    for g in range(2):
        for t in range(2):
            for m in range(2):
                do_copies.append(
                    pltpu.make_async_copy(
                        dog.at[pl.ds(t * QT, QT), pl.ds((2 * g + m) * HEAD, HEAD)],
                        do.at[g, t, pl.ds(m * QT, QT), :],
                        sem_do.at[4 * g + 2 * t + m],
                    )
                )
    for copy in do_copies:
        copy.start()

    first = ctx * TOK
    lane = lax.broadcasted_iota(jnp.int32, (1, TOK), 1)
    low = jnp.maximum(doc[...].reshape(1, TOK) - first + WINDOW, lane + 1)
    for t in range(2):
        part = low[:, t * QT : (t + 1) * QT] - t * QT
        lo[t] = jnp.concatenate([part, part], axis=1)

    def send_kv(g, j, half, far):
        if far:
            source, rows, device = 2 * TOK, 0, next2
        else:
            source, rows, device = pl.multiple_of(2 * TOK * (1 - odd), TOK), TOK, pair
        return pltpu.make_async_remote_copy(
            src_ref=kv.at[g, j, pl.ds(source, TOK), :],
            dst_ref=kv.at[g, j, pl.ds(rows, TOK), :],
            send_sem=kv_ss.at[g, j, half, far],
            recv_sem=kv_rs.at[g, j, half, far],
            device_id=device,
            device_id_type=MESH,
        )

    def relay_kv(g, j):
        for half in range(1):
            send_kv(g, j, half, 1).wait_recv()
            send_kv(g, j, half, 0).start()

    for g in range(2):
        acc[:, pl.ds(0, 256)] = jnp.zeros((TOK, 256), F32)

        @pl.loop(0, kcn)
        def _(k):
            if g == 0:
                in_h(k).wait()
            in_k(g, k).wait()
            in_v(g, k).wait()
            acc[:, pl.ds(0, 256)] += jnp.dot(
                h[k], wall[cols(k), pl.ds(512 + 256 * g, 256)], preferred_element_type=F32
            )

        for j in range(2):
            kv[g, j, pl.ds(2 * TOK, TOK), :] = acc[:, pl.ds(j * HEAD, HEAD)].astype(BF16)
        if g == 0:
            pl.semaphore_wait(barrier, 5)
        for j in range(2):
            for half in range(1):
                send_kv(g, j, half, 1).start()

                @pl.when(odd == 0)
                def _():
                    send_kv(g, j, half, 0).start()

    acc[...] = jnp.zeros_like(acc)

    @pl.loop(0, kcn)
    def _(k):
        in_q(k).wait()
        acc[...] += jnp.dot(h[k], wall[cols(k), pl.ds(0, 512)], preferred_element_type=F32)

    for g in range(2):
        for t in range(2):
            for m in range(2):
                q[g, t, pl.ds(m * QT, QT), :] = acc[
                    pl.ds(t * QT, QT), pl.ds((2 * g + m) * HEAD, HEAD)
                ].astype(BF16)
    for copy in do_copies:
        copy.wait()

    def same(a, b):
        return 1 - (a + b - 2 * a * b)

    def place(b):
        return pl.multiple_of(64 * (2 * same(lax.rem(b, 2), core) + same(b // 2, zpos)), 64)

    def send_dkv(g, j, half, far):
        return pltpu.make_async_remote_copy(
            src_ref=dkv_out.at[g, j, 1 - far, :, half],
            dst_ref=dkv_in.at[far, g, j, :, half],
            send_sem=dkv_ss.at[g, j, half, far],
            recv_sem=dkv_rs.at[g, j, half, far],
            device_id=prev2 if far else pair,
            device_id_type=MESH,
        )

    def relay_dkv(g, j, half):
        send_dkv(g, j, half, 0).wait_recv()
        dkv_out[g, j, 0, :, half] = (
            dkv_out[g, j, 0, :, half].astype(F32) + dkv_in[0, g, j, :, half].astype(F32)
        ).astype(BF16)
        send_dkv(g, j, half, 1).start()

    @pl.when(odd == 1)
    def _():
        for j in range(2):
            relay_kv(0, j)

    @pl.loop(0, 2)
    def _(g):
        @pl.when(odd == 0)
        def _():
            for j in range(2):
                for half in range(1):
                    send_kv(g, j, half, 1).wait_recv()

        for j in range(2):
            for half in range(1):
                send_kv(g, j, half, 0).wait_recv()
        for t in range(2):
            lowest = lo[t]
            local = lax.broadcasted_iota(jnp.int32, (CH, 2 * QT), 0)

            def chunk(c):
                return pl.ds(c * CH, CH)

            def keys(j, c):
                return kv[g, j, pl.ds((t + c) * CH, CH), :]

            top = None
            for c in range(5):
                kept = lax.dot_general(keys(0, c), q[g, t], NT, preferred_element_type=F32)
                allowed = local >= lowest - c * CH
                if c == 4:
                    lane2 = lax.broadcasted_iota(jnp.int32, (1, QT), 1)
                    allowed = allowed & (local <= jnp.concatenate([lane2, lane2], axis=1))
                kept = jnp.where(allowed, kept, -jnp.inf)
                s[chunk(c), :] = kept
                here = jnp.max(kept, axis=0, keepdims=True)
                top = here if top is None else jnp.maximum(top, here)

            total, dots = 0.0, 0.0
            for c in range(5):
                grads = lax.dot_general(keys(1, c), do[g, t], NT, preferred_element_type=F32)
                weight = jnp.exp2((s[chunk(c), :] - top) * (SCALE * LOG2E))
                s[chunk(c), :] = weight
                dp[chunk(c), :] = grads
                total = total + jnp.sum(weight, axis=0, keepdims=True)
                dots = dots + jnp.sum(weight * grads, axis=0, keepdims=True)
            inverse = 1.0 / total
            row_dot = dots * inverse

            for c in range(5):
                prob = s[chunk(c), :] * inverse
                low_prob = prob.astype(BF16)
                d_score = (prob * (dp[chunk(c), :] - row_dot)).astype(BF16)
                ds[g, t, chunk(c), :] = d_score
                if t + c < 4:
                    rows = pl.ds((t + c) * CH, CH)
                    d_key = jnp.dot(d_score, q[g, t], preferred_element_type=F32)
                    d_val = jnp.dot(low_prob, do[g, t], preferred_element_type=F32)
                    if t == 1:
                        d_key = d_key + dkv[g, 0, rows, :]
                        d_val = d_val + dkv[g, 1, rows, :]
                    if t == 1 or c == 0:
                        blocks = pl.ds(2 * ((t + c) % 2), 2)
                        split = (2, 2, 64, HEAD)
                        dkv_out[g, 0, (t + c) // 2, blocks] = (d_key * SCALE).astype(BF16).reshape(split)
                        dkv_out[g, 1, (t + c) // 2, blocks] = d_val.astype(BF16).reshape(split)
                    else:
                        dkv[g, 0, rows, :] = d_key
                        dkv[g, 1, rows, :] = d_val
                else:
                    pw[g, c - 4 if t == 0 else c - 2] = low_prob

            @pl.when((odd == 1) & (g == 0))
            def _():
                relay_kv(1, t)

        for half in range(2):
            for j in range(2):
                send_dkv(g, j, half, 0).start()

                @pl.when(odd == 0)
                def _():
                    send_dkv(g, j, half, 1).start()

    @pl.loop(0, 2)
    def _(g):
        for t in range(2):
            dq = lax.dot_general(
                kv[g, 0, pl.ds(t * QT, KEYS), :], ds[g, t], TN, preferred_element_type=F32
            )
            dq = jnp.transpose(dq * SCALE).astype(BF16)
            for m in range(2):
                feats = pl.ds(pl.multiple_of((2 * g + m) * HEAD, HEAD), HEAD)
                for j in range(2):
                    for half in range(2):
                        start = m * QT + j * 128 + half * 64
                        grad[half, pl.ds(place(2 * t + j), 64), feats] = dq[start : start + 64]

        def own(j, first_low, second_low, third_low, by):
            dkv[g, j, pl.ds(4 * CH, CH), :] = jnp.dot(
                first_low, by[g, 0], preferred_element_type=F32
            ) + jnp.dot(second_low, by[g, 1], preferred_element_type=F32)
            dkv[g, j, pl.ds(5 * CH, CH), :] = jnp.dot(third_low, by[g, 1], preferred_element_type=F32)

        last = pl.ds(4 * CH, CH)
        own(0, ds[g, 0, last, :], ds[g, 1, pl.ds(3 * CH, CH), :], ds[g, 1, last, :], q)
        own(1, pw[g, 0], pw[g, 1], pw[g, 2], do)

    @pl.when(odd == 1)
    def _():
        for g in range(2):
            for half in range(2):
                for j in range(2):
                    relay_dkv(g, j, half)

    def send_r1(half, c):
        return pltpu.make_async_remote_copy(
            src_ref=rs1_out.at[half, c], dst_ref=rs1_in.at[half, c],
            send_sem=r1_ss.at[half, c], recv_sem=r1_rs.at[half, c],
            device_id=mate, device_id_type=MESH,
        )

    def out_cols(c):
        return pl.ds(pl.multiple_of(c * nc, nc), nc)

    def out_rows(half):
        return pl.ds(pl.multiple_of(half * 64, 64), 64)

    def send_r2(half, c):
        return pltpu.make_async_remote_copy(
            src_ref=rs2_out.at[half, c], dst_ref=rs2_in.at[out_rows(half), out_cols(c)],
            send_sem=r2_ss.at[half, c], recv_sem=r2_rs.at[half, c],
            device_id=across, device_id_type=MESH,
        )

    def join(half, c):
        send_r1(half, c).wait_recv()
        rs2_out[half, c] = (other[c] + rs1_in[half, c, pl.ds(0, 64), :].astype(F32)).astype(BF16)
        send_r2(half, c).start()
        keep[out_rows(half), out_cols(c)] += rs1_in[half, c, pl.ds(64, 64), :].astype(F32)

    @pl.loop(0, 2)
    def _(half):
        for g in range(2):
            for j in range(2):
                @pl.when(odd == 0)
                def _():
                    send_dkv(g, j, half, 0).wait_recv()

                send_dkv(g, j, half, 1).wait_recv()
                for b in range(4):
                    own = dkv[g, j, pl.ds(pl.multiple_of(2 * TOK + b * 128 + half * 64, 64), 64), :]
                    if j == 0:
                        own = own * SCALE
                    near = jnp.where(odd == 0, dkv_in[0, g, j, b, half].astype(F32), 0.0)
                    whole = own + (near + dkv_in[1, g, j, b, half].astype(F32))
                    grad[half, pl.ds(place(b), 64), pl.ds(512 + g * 256 + j * HEAD, HEAD)] = whole.astype(BF16)

        @pl.loop(0, ncn)
        def _(c):
            part = lax.dot_general(
                grad[half], wall[out_cols(c), :], NT, preferred_element_type=F32
            )
            rs1_out[half, c] = part[:128].astype(BF16)
            send_r1(half, c).start()

            @pl.when(c > 0)
            def _():
                join(half, c - 1)

            other[c] = part[128:192]
            keep[out_rows(half), out_cols(c)] = part[192:]

        join(half, ncn - 1)

    for g in range(2):
        for j in range(2):
            for half in range(2):
                for far in range(2):
                    if half == 0:
                        send_kv(g, j, half, far).wait_send()
                    send_dkv(g, j, half, far).wait_send()

    @pl.loop(0, ncn)
    def _(c):
        for half in range(2):
            send_r1(half, c).wait_send()
            send_r2(half, c).wait_send()
            send_r2(half, c).wait_recv()


def shards(hidden, w_query, key_weight, value_weight, out_gradient, doc_start, *, n_ctx):
    width = hidden.shape[1]
    kcn = 7
    kc = width // kcn
    nc = 256
    ncn = width // nc
    dma = pltpu.SemaphoreType.DMA
    anywhere = pl.BlockSpec(memory_space=pl.ANY)
    own, across = pl.pallas_call(
        functools.partial(kernel, n_ctx, kcn, kc, ncn, nc),
        out_shape=(
            pltpu.VMEM((128, width), F32),
            pltpu.VMEM((128, width), BF16),
        ),
        in_specs=[anywhere] * 5 + [pl.BlockSpec(memory_space=pltpu.VMEM)],
        out_specs=(pl.BlockSpec(memory_space=pltpu.VMEM),) * 2,
        scratch_shapes=[
            pltpu.VMEM((kcn, TOK, kc), BF16),
            pltpu.VMEM((width, 1024), BF16),
            pltpu.VMEM((TOK, TOK), F32),
            pltpu.VMEM((2, 2, 3 * TOK, HEAD), BF16),
            pltpu.VMEM((2, 2, 2 * QT, HEAD), BF16),
            pltpu.VMEM((2, 2, 2 * QT, HEAD), BF16),
            pltpu.VMEM((2, 1, 2 * QT), jnp.int32),
            pltpu.VMEM((KEYS, 2 * QT), F32),
            pltpu.VMEM((KEYS, 2 * QT), F32),
            pltpu.VMEM((2, 3, CH, 2 * QT), BF16),
            pltpu.VMEM((2, 2, KEYS, 2 * QT), BF16),
            pltpu.VMEM((2, 2, 3 * TOK, HEAD), F32),
            pltpu.VMEM((2, 2, 2, 4, 2, 64, HEAD), BF16),
            pltpu.VMEM((2, 2, 2, 4, 2, 64, HEAD), BF16),
            pltpu.VMEM((2, QT, 1024), BF16),
            pltpu.VMEM((2, ncn, 128, nc), BF16),
            pltpu.VMEM((2, ncn, 128, nc), BF16),
            pltpu.VMEM((2, ncn, 64, nc), BF16),
            pltpu.VMEM((ncn, 64, nc), F32),
            dma((kcn,)), dma((2, kcn)), dma((2, kcn)), dma((kcn,)), dma((8,)),
            dma((2, 2, 2, 2)), dma((2, 2, 2, 2)), dma((2, 2, 2, 2)), dma((2, 2, 2, 2)),
            dma((2, ncn)), dma((2, ncn)), dma((2, ncn)), dma((2, ncn)),
        ],
        compiler_params=pltpu.CompilerParams(
            collective_id=0, has_side_effects=True, vmem_limit_bytes=60 * 1024 * 1024
        ),
    )(hidden, w_query, key_weight, value_weight, out_gradient, doc_start)
    return own + across.astype(F32)


def solution(mesh):
    in_specs = (
        P("ctx", None),
        P(None, "head"),
        P(None, "head"),
        P(None, "head"),
        P("ctx", "head"),
        P("ctx"),
    )
    out_specs = P(("ctx", "head"), None)
    return jax.shard_map(
        functools.partial(shards, n_ctx=mesh.shape["ctx"]),
        mesh=mesh, in_specs=in_specs, out_specs=out_specs, check_vma=False,
    )
```
